32 devices in a mesh: group: 2 (over x), ctx: 16 (over z, y, core).
Axes of the slice: x: 2, y: 2, z: 4, core: 2. Of those that a mesh axis runs over, the one named last changes fastest.
Arguments:
- query_proj: bfloat16 [8192, 2048], P(('group', 'ctx')), parts along dimension 0, may hold values from -6 to 6
- key_proj: bfloat16 [8192, 2048], P(('group', 'ctx')), parts along dimension 0, may hold values from -6 to 6
- value_proj: bfloat16 [8192, 2048], P(('group', 'ctx')), parts along dimension 0, may hold values from -6 to 6
- short_weight: float32 [3, 3, 2048], replicated, may hold values from -3.5 to 3.5
- decay_rate: float32 [16, 2048], replicated, may hold values from 4.8828125e-05 to 0.125
- residue: float32 [16, 2048], replicated, may hold values from -0.5 to 0.5
- skip_gain: float32 [2048], replicated, may hold values from -4 to 4
Outputs:
- mixed: bfloat16 [8192, 2048], P(('group', 'ctx')), parts along dimension 0
The draws below stay inside these ranges and needn't reach their ends.
There are 2 independent parts, one for each index of `group`. The reference program is written for one: setup_inputs(seed, part) draws one part's arguments, and reference() takes and returns one part's arrays. A program takes and returns all parts, laid end to end along the dimension named above; an argument that names none is the same for every part. Nothing has to cross between parts.
All inputs are finite; a program needn't handle non-finite values.
Results may differ from the reference program's by a relative error of at most 0.001.
Values may be sent and summed in bfloat16 or wider, within the bound.
A program may use at most 128 MiB of HBM per device.

```python
import math
import jax
import jax.numpy as jnp
from jax import lax

C = 2048
ORDER = 16
SHORT = 3
SEQ = 4096


def modal_pair(key):
    base = jax.random.fold_in(key, 1301)
    flag_key = jax.random.fold_in(base, 1)
    rate_key = jax.random.fold_in(base, 2)
    weight_key = jax.random.fold_in(base, 3)
    fast_key = jax.random.fold_in(base, 4)
    slow_flag = jax.random.randint(flag_key, (1, C), 0, 2)
    slow_rate = jnp.exp(jax.random.uniform(rate_key, (ORDER, C), jnp.float32, math.log(0.3 / SEQ), math.log(2.0 / SEQ)))
    fast_rate = jnp.exp(jax.random.uniform(fast_key, (ORDER, C), jnp.float32, math.log(1.0 / 50.0), math.log(0.125)))
    rate = jnp.where(slow_flag == 1, slow_rate, fast_rate)
    normed = jax.random.truncated_normal(weight_key, -4.0, 4.0, (ORDER, C), jnp.float32)
    weight = normed * jnp.sqrt(2.0 * rate / ORDER)
    return (rate, weight)


def draw_decay_rate(key, part):
    rate, weight = modal_pair(key)
    return rate


def draw_residue(key, part):
    rate, weight = modal_pair(key)
    return weight


def block_scale(own_key, extent, cuts, least, largest):
    level = 1.0
    for axis_at, parts in cuts:
        heights = jax.random.uniform(jax.random.fold_in(jax.random.fold_in(own_key, 6), axis_at), (parts,), jnp.float32, least / len(cuts), largest / len(cuts))
        level = level * jnp.repeat(jnp.exp(heights), extent[axis_at] // parts).reshape((-1,) + (1,) * (len(extent) - 1 - axis_at))
    return level


def noise(key, shape, deviation, bound, cuts=(), dtype=jnp.bfloat16):
    values = deviation * jax.random.normal(key, shape, jnp.float32)
    if cuts:
        values = values * block_scale(key, shape, cuts, -0.22, 0.18)
    return jnp.clip(values, -bound, bound).astype(dtype)


def setup_inputs(seed: int = 0, part: int = 0) -> dict:
    key_list = jax.random.split(jax.random.key(seed), 8)
    part_keys = jax.random.split(jax.random.fold_in(key_list[7], part), 8)
    return {
        "query_proj": noise(part_keys[0], (SEQ, C), 1.0, 6.0, ((0, 16),)),
        "key_proj": noise(part_keys[1], (SEQ, C), 1.0, 6.0, ((0, 16),)),
        "value_proj": noise(part_keys[2], (SEQ, C), 1.0, 6.0, ((0, 16),)),
        "short_weight": noise(key_list[3], (3, SHORT, C), SHORT ** -0.5, 3.5, (), jnp.float32),
        "decay_rate": draw_decay_rate(jax.random.fold_in(key_list[7], 71), part),
        "residue": draw_residue(jax.random.fold_in(key_list[7], 71), part),
        "skip_gain": noise(key_list[6], (C,), 1.0, 4.0, (), jnp.float32),
    }


def causal_short(rows, weights):
    taps = weights.shape[0]
    length = rows.shape[0]
    padding = jnp.zeros((taps - 1, rows.shape[1]), jnp.float32)
    extended = jnp.concatenate([padding, rows.astype(jnp.float32)], axis=0)
    total = weights[0] * extended[taps - 1:]
    for lag in range(1, taps):
        total = total + weights[lag] * extended[taps - 1 - lag: taps - 1 - lag + length]
    return total


def reference(query_proj, key_proj, value_proj, short_weight, decay_rate, residue, skip_gain):
    query_conv = causal_short(query_proj, short_weight[0])
    key_conv = causal_short(key_proj, short_weight[1])
    value_conv = causal_short(value_proj, short_weight[2])
    gated = key_conv * value_conv
    times = jnp.arange(SEQ).astype(jnp.float32)

    def add_mode(total, pair):
        rate, weight = pair
        return total + weight * jnp.exp(-rate * times[:, None]), None

    response, unused = lax.scan(add_mode, jnp.zeros((SEQ, C), jnp.float32), (decay_rate, residue))
    spectra = jnp.fft.rfft(gated, n=2 * SEQ, axis=0) * jnp.fft.rfft(response, n=2 * SEQ, axis=0)
    conv = jnp.fft.irfft(spectra, n=2 * SEQ, axis=0)[:SEQ]
    return (query_conv * (conv + skip_gain * gated)).astype(jnp.bfloat16)
```

```python
import functools

import jax
import jax.numpy as jnp
from jax import lax
from jax.experimental import pallas as pl
from jax.experimental.pallas import tpu as pltpu
from jax.sharding import PartitionSpec as P

MESH = pl.DeviceIdType.MESH
F32 = jnp.float32
BF16 = jnp.bfloat16
LANES = 128
SUBS = 8
WIDE = SUBS * LANES
CHUNK = 8
EDGE = 16


def owning(parts):
    return parts // 4, parts // 2


def tree_sum(terms):
    terms = list(terms)
    while len(terms) > 1:
        half = len(terms) // 2
        rest = terms[2 * half :]
        terms = [terms[i] + terms[i + half] for i in range(half)] + rest
    return terms[0]


def layer_kernel(
    parts, q_hbm, k_hbm, v_hbm, sw_hbm, rate_hbm, res_hbm, skip_hbm, out_ref,
    qbuf, kbuf, vbuf, edge, sw, rate, res, skip,
    perm, qx, kx, vx, tail, halo, sw_t, rate_t, res_t, skip_t,
    a1, a6, a8, a248, a256, w_s, taps, g_s, h_s, y_s, qc_s, o_s,
    ends, got, back, inc,
    load_sem, edge_sem, par_sem, halo_sem, send_a, recv_a, send_b, recv_b,
):
    tokens, channels = qbuf.shape
    modes = rate.shape[0]
    halves = channels // WIDE
    first, owners = owning(parts)
    own = modes // owners
    last = parts - 1
    chunks = tokens // CHUNK
    pairs = chunks // 2
    span = tokens + 2
    block = perm.shape[0] // SUBS
    stage = 2 * block
    stages = tokens // stage
    me = lax.axis_index("ctx")
    owning_here = jnp.logical_and(me >= first, me < first + owners)
    barrier = pltpu.get_barrier_semaphore()

    def row(i, count=1):
        start = i * SUBS
        if not isinstance(start, int):
            start = pl.multiple_of(start, SUBS)
        return pl.ds(start, count * SUBS)

    edge_copies = []
    for m, src in enumerate((q_hbm, k_hbm, v_hbm)):
        edge_copies.append(pltpu.make_async_copy(src.at[pl.ds(tokens - EDGE, EDGE)], edge.at[m], edge_sem.at[m]))
    par_copies = []
    for i, (src, dst) in enumerate(((rate_hbm, rate), (res_hbm, res), (sw_hbm, sw), (skip_hbm, skip))):
        par_copies.append(pltpu.make_async_copy(src, dst, par_sem.at[i]))
    loads = {}
    order = []

    def load(m, src, dst, h, part, first, count):
        at = (pl.ds(first, count), pl.ds(h * WIDE, WIDE))
        loads[m, h, part] = pltpu.make_async_copy(src.at[at], dst.at[at], load_sem.at[len(order)])
        order.append(loads[m, h, part])

    for h in range(halves):
        for part, begin, count in ((0, 0, stage), (1, stage, tokens - stage)):
            load(1, k_hbm, kbuf, h, part, begin, count)
            load(2, v_hbm, vbuf, h, part, begin, count)
    for h in range(halves):
        load(0, q_hbm, qbuf, h, 0, 0, tokens)
    for c in edge_copies + par_copies + order:
        c.start()

    halo[...] = jnp.zeros(halo.shape, F32)
    inc[...] = jnp.zeros(inc.shape, F32)

    def greet(peer, carry=0):
        @pl.when(peer != me)
        def _():
            pl.semaphore_signal(barrier, inc=1, device_id={"ctx": peer}, device_id_type=MESH)

        return carry

    def owns(x):
        return jnp.logical_and(x >= first, x < first + owners)

    lax.fori_loop(jnp.where(owning_here, 0, first), jnp.where(owning_here, parts, first + owners), greet, 0)

    @pl.when(jnp.logical_and(jnp.logical_not(owning_here), jnp.logical_and(me > 0, jnp.logical_not(owns(me - 1)))))
    def _():
        greet(me - 1)

    row_id = lax.broadcasted_iota(jnp.int32, perm.shape, 0)
    col_id = lax.broadcasted_iota(jnp.int32, perm.shape, 1)
    perm[...] = jnp.where(col_id == (row_id % SUBS) * block + row_id // SUBS, 1.0, 0.0).astype(BF16)
    for dst in (qx, kx, vx):
        for h in range(halves):
            dst[row(h * span, 2), :] = jnp.zeros((2 * SUBS, LANES), F32)

    for c in edge_copies:
        c.wait()
    for m in range(3):
        for h in range(halves):
            for s in range(SUBS):
                at = (h * SUBS + s) * LANES
                rows = edge[m, :, at : at + LANES].astype(F32)
                tail[pl.ds((m * halves + h) * 2 * SUBS + s, 2, stride=SUBS), :] = rows[EDGE - 2 :, :]

    for c in par_copies:
        c.wait()
    for h in range(halves):
        for s in range(SUBS):
            at = (h * SUBS + s) * LANES
            cols = slice(at, at + LANES)
            rate_t[pl.ds(h * modes * SUBS + s, modes, stride=SUBS), :] = rate[:, cols]
            res_t[pl.ds(h * modes * SUBS + s, modes, stride=SUBS), :] = res[:, cols]
            for m in range(3):
                sw_t[pl.ds((h * 3 + m) * 3 * SUBS + s, 3, stride=SUBS), :] = sw[m, :, cols]
            skip_t[h * SUBS + s : h * SUBS + s + 1, :] = skip[0:1, cols]

    def constants(h, carry):
        zero_lag, sums = [], [[] for _ in range(CHUNK)]
        for n in range(modes):
            at = row(h * modes + n)
            negative = -rate_t[at, :]
            weight = res_t[at, :]
            one = jnp.exp(negative)
            a1[at, :] = one
            a6[at, :] = jnp.exp(negative * float(CHUNK - 2))
            a8[at, :] = jnp.exp(negative * float(CHUNK))
            a248[at, :] = jnp.exp(negative * float(tokens - CHUNK))
            a256[at, :] = jnp.exp(negative * float(tokens))
            zero_lag.append(weight)
            for i in range(CHUNK):
                weight = weight * one
                w_s[row((h * CHUNK + i) * modes + n), :] = weight
                sums[i].append(weight)
        taps[row(h * CHUNK), :] = tree_sum(zero_lag) + skip_t[row(h), :]
        for d in range(1, CHUNK):
            taps[row(h * CHUNK + d), :] = tree_sum(sums[d - 1])
        return carry

    lax.fori_loop(0, halves, constants, 0)

    halo_copy = pltpu.make_async_remote_copy(
        src_ref=tail, dst_ref=halo, send_sem=halo_sem.at[0], recv_sem=halo_sem.at[1],
        device_id={"ctx": lax.rem(me + 1, parts)}, device_id_type=MESH,
    )

    def open_halo():
        to_next = jnp.logical_and(me < last, jnp.logical_not(owns(me + 1)))
        pl.semaphore_wait(barrier, jnp.where(owning_here, last, owners + jnp.where(to_next, 1, 0)))

        @pl.when(me < last)
        def _():
            halo_copy.start()

    def spread(buf, dst, h, at):
        t = at * stage
        source = jnp.minimum(h, halves - 1) if not isinstance(h, int) else min(h, halves - 1)
        sides = []
        for u in (0, block):
            rows = pl.ds(t + u if isinstance(t, int) else pl.multiple_of(t + u, block), block)
            pieces = []
            for s in range(SUBS):
                lane = source * WIDE + s * LANES
                pieces.append(buf[rows, pl.ds(lane if isinstance(lane, int) else pl.multiple_of(lane, LANES), LANES)])
            sides.append(jnp.concatenate(pieces, axis=0))
        moved = jnp.dot(perm[...], jnp.concatenate(sides, axis=1), preferred_element_type=F32)
        base = h * span + 2 + t
        dst[row(base, block), :] = moved[:, :LANES]
        dst[row(base + block, block), :] = moved[:, LANES:]

    def following(h, at):
        last = at == stages - 1
        return jnp.where(last, h + 1, h), jnp.where(last, 0, at + 1)

    def filtered(ref, m, h, t, count):
        base = h * span + t
        x = [ref[row(base + i), :] for i in range(count + 2)]
        w = [sw_t[row((h * 3 + m) * 3 + lag), :] for lag in range(3)]
        return [w[0] * x[i + 2] + w[1] * x[i + 1] + w[2] * x[i] for i in range(count)]

    def states(h):
        ends[row(h * modes, modes), :] = jnp.zeros((modes * SUBS, LANES), F32)

        def step(at, carry):
            @pl.when(at == 0)
            def _():
                loads[1, h, 1].wait()
                loads[2, h, 1].wait()

            if h + 1 < halves:
                @pl.when(at == stages - 1)
                def _():
                    loads[1, h + 1, 0].wait()
                    loads[2, h + 1, 0].wait()

            total = [ends[row(h * modes + n), :] for n in range(modes)]
            for p in range(stage // (2 * CHUNK)):
                t = at * stage + p * 2 * CHUNK
                kc = filtered(kx, 1, h, t, 2 * CHUNK)
                vc = filtered(vx, 2, h, t, 2 * CHUNK)
                g = [a * b for a, b in zip(kc, vc)]
                for i in range(2 * CHUNK):
                    g_s[row(h * tokens + t + i), :] = g[i]
                for n in range(modes):
                    a = a1[row(h * modes + n), :]
                    factor = a8[row(h * modes + n), :]
                    for c in range(2):
                        local = g[c * CHUNK]
                        for i in range(1, CHUNK):
                            local = a * local + g[c * CHUNK + i]
                        h_s[row((h * chunks + t // CHUNK + c) * modes + n), :] = local
                        total[n] = factor * total[n] + local
            for n in range(modes):
                ends[row(h * modes + n), :] = total[n]
            nh, na = following(h, at)
            spread(kbuf, kx, nh, na)
            spread(vbuf, vx, nh, na)
            return carry

        lax.fori_loop(0, stages, step, 0)

    def margin(dst, m, h):
        dst[row(h * span, 2), :] = halo[row((m * halves + h) * 2, 2), :]

    def correct(h):
        margin(kx, 1, h)
        margin(vx, 2, h)
        g = [a * b for a, b in zip(filtered(kx, 1, h, 0, 2), filtered(vx, 2, h, 0, 2))]
        change = [g[i] - g_s[row(h * tokens + i), :] for i in range(2)]
        for i in range(2):
            g_s[row(h * tokens + i), :] = g[i]
        for n in range(modes):
            at = row(h * modes + n)
            extra = a6[at, :] * (a1[at, :] * change[0] + change[1])
            first = row(h * chunks * modes + n)
            h_s[first, :] = h_s[first, :] + extra
            ends[at, :] = ends[at, :] + a248[at, :] * extra

    def modes_of(h, owner):
        return row(h * modes + (owner - first) * own, own)

    def sums(h, device):
        return row((h * parts + device) * own, own)

    def send_ends(h, owner):
        return pltpu.make_async_remote_copy(
            src_ref=ends.at[modes_of(h, owner)], dst_ref=got.at[sums(h, me)],
            send_sem=send_a.at[h * owners + owner - first], recv_sem=recv_a.at[h * parts + me],
            device_id={"ctx": owner}, device_id_type=MESH,
        )

    def got_ends(h, p):
        return pltpu.make_async_remote_copy(
            src_ref=ends.at[modes_of(h, first)], dst_ref=got.at[sums(h, p)],
            send_sem=send_a.at[h * owners], recv_sem=recv_a.at[h * parts + p],
            device_id={"ctx": p}, device_id_type=MESH,
        )

    def send_back(h, q):
        return pltpu.make_async_remote_copy(
            src_ref=back.at[sums(h, q)], dst_ref=inc.at[modes_of(h, me)],
            send_sem=send_b.at[h * parts + q], recv_sem=recv_b.at[h * owners + me - first],
            device_id={"ctx": q}, device_id_type=MESH,
        )

    def got_back(h, owner):
        return pltpu.make_async_remote_copy(
            src_ref=back.at[sums(h, 0)], dst_ref=inc.at[modes_of(h, owner)],
            send_sem=send_b.at[h * parts], recv_sem=recv_b.at[h * owners + owner - first],
            device_id={"ctx": owner}, device_id_type=MESH,
        )

    def share(h):
        def body(i, carry):
            owner = first + lax.rem(me + i, owners)

            @pl.when(owner != me)
            def _():
                send_ends(h, owner).start()

            return carry

        @pl.when(me < last)
        def _():
            lax.fori_loop(0, owners, body, 0)

        @pl.when(owning_here)
        def _():
            got[sums(h, me), :] = ends[modes_of(h, me), :]

    def took(h):
        factor = a256[modes_of(h, me), :]

        def body(p, total):
            @pl.when(p != me)
            def _():
                got_ends(h, p).wait_recv()

            total = factor * total + got[sums(h, p), :]
            q = p + 1

            @pl.when(q != me)
            def _():
                back[sums(h, q), :] = total
                send_back(h, q).start()

            @pl.when(q == me)
            def _():
                inc[modes_of(h, me), :] = total

            return total

        lax.fori_loop(0, last, body, jnp.zeros((own * SUBS, LANES), F32))

    def local(h):
        def step(at, carry):
            if h + 1 < halves:
                @pl.when(at == stages - 1)
                def _():
                    loads[0, h + 1, 0].wait()

            tap = [taps[row(h * CHUNK + d), :] for d in range(CHUNK)]
            for c in range(stage // CHUNK):
                t = at * stage + c * CHUNK
                qc = filtered(qx, 0, h, t, CHUNK)
                base = h * tokens + t
                g = [g_s[row(base + i), :] for i in range(CHUNK)]
                for i in range(CHUNK):
                    y_s[row(base + i), :] = tree_sum(tap[d] * g[i - d] for d in range(i + 1))
                    qc_s[row(base + i), :] = qc[i]
            nh, na = following(h, at)
            spread(qbuf, qx, nh, na)
            return carry

        lax.fori_loop(0, stages, step, 0)

    def convert(h, pair):
        t = pair * 2 * CHUNK
        for s in range(SUBS):
            at = (h * SUBS + s) * LANES
            base = (h * tokens + t) * SUBS + s
            value = o_s[pl.ds(base, 2 * CHUNK, stride=SUBS), :]
            out_ref[pl.ds(pl.multiple_of(t, 2 * CHUNK), 2 * CHUNK), at : at + LANES] = value.astype(BF16)

    def finish(h):
        def waits(i, carry):
            owner = first + i

            @pl.when(owner != me)
            def _():
                got_back(h, owner).wait_recv()

            return carry

        @pl.when(me > 0)
        def _():
            lax.fori_loop(0, owners, waits, 0)

        def step(pair, carry):
            t = pair * 2 * CHUNK
            entry = [list(carry), [], []]
            for c in range(2):
                for n in range(modes):
                    entry[c + 1].append(
                        a8[row(h * modes + n), :] * entry[c][n] + h_s[row((h * chunks + pair * 2 + c) * modes + n), :]
                    )
            for i in range(CHUNK):
                w = [w_s[row((h * CHUNK + i) * modes + n), :] for n in range(modes)]
                for c in range(2):
                    at = row(h * tokens + t + c * CHUNK + i)
                    o_s[at, :] = qc_s[at, :] * (
                        y_s[at, :] + tree_sum(w[n] * entry[c][n] for n in range(modes))
                    )
            convert(h, pair)
            return tuple(entry[2])

        lax.fori_loop(0, pairs, step, tuple(inc[row(h * modes + n), :] for n in range(modes)))

    loads[1, 0, 0].wait()
    loads[2, 0, 0].wait()
    spread(kbuf, kx, 0, 0)
    spread(vbuf, vx, 0, 0)
    states(0)
    open_halo()
    for h in range(1, halves):
        states(h)

    @pl.when(me > 0)
    def _():
        halo_copy.wait_recv()

    for h in range(halves):
        correct(h)
        share(h)
    loads[0, 0, 0].wait()
    spread(qbuf, qx, 0, 0)
    for h in range(halves):
        margin(qx, 0, h)
    for h in range(halves):
        local(h)

    @pl.when(owning_here)
    def _():
        for h in range(halves):
            took(h)

    for h in range(halves):
        finish(h)

    @pl.when(me < last)
    def _():
        halo_copy.wait_send()

    def sent_ends(i, carry):
        owner = first + i

        @pl.when(owner != me)
        def _():
            for h in range(halves):
                send_ends(h, owner).wait_send()

        return carry

    def sent_back(q, carry):
        @pl.when(q != me)
        def _():
            for h in range(halves):
                send_back(h, q).wait_send()

        return carry

    @pl.when(me < last)
    def _():
        lax.fori_loop(0, owners, sent_ends, 0)

    @pl.when(owning_here)
    def _():
        lax.fori_loop(1, parts, sent_back, 0)


def per_device(query_proj, key_proj, value_proj, short_weight, decay_rate, residue, skip_gain):
    parts = lax.axis_size("ctx")
    tokens, channels = query_proj.shape
    modes = decay_rate.shape[0]
    halves = channels // WIDE
    owners = owning(parts)[1]
    own = modes // owners
    any_space = pl.BlockSpec(memory_space=pltpu.HBM)
    vm = pltpu.VMEM
    dma = pltpu.SemaphoreType.DMA

    def regs(count):
        return vm((count * SUBS, LANES), F32)

    return pl.pallas_call(
        functools.partial(layer_kernel, parts),
        out_shape=pltpu.VMEM((tokens, channels), BF16),
        in_specs=[any_space] * 7,
        out_specs=pl.BlockSpec(memory_space=pltpu.VMEM),
        scratch_shapes=[
            vm((tokens, channels), BF16),
            vm((tokens, channels), BF16),
            vm((tokens, channels), BF16),
            vm((3, EDGE, channels), BF16),
            vm(short_weight.shape, F32),
            vm(decay_rate.shape, F32),
            vm(residue.shape, F32),
            vm((1, channels), F32),
            vm((256, 256), BF16),
            regs((halves + 1) * (tokens + 2)),
            regs((halves + 1) * (tokens + 2)),
            regs((halves + 1) * (tokens + 2)),
            regs(3 * halves * 2),
            regs(3 * halves * 2),
            regs(halves * 9),
            regs(halves * modes),
            regs(halves * modes),
            regs(halves),
            regs(halves * modes),
            regs(halves * modes),
            regs(halves * modes),
            regs(halves * modes),
            regs(halves * modes),
            regs(halves * CHUNK * modes),
            regs(halves * CHUNK),
            regs(halves * tokens),
            regs(halves * tokens // CHUNK * modes),
            regs(halves * tokens),
            regs(halves * tokens),
            regs(halves * tokens),
            regs(halves * modes),
            regs(halves * parts * own),
            regs(halves * parts * own),
            regs(halves * modes),
            dma((5 * halves,)),
            dma((3,)),
            dma((4,)),
            dma((2,)),
            dma((halves * owners,)),
            dma((halves * parts,)),
            dma((halves * parts,)),
            dma((halves * owners,)),
        ],
        compiler_params=pltpu.CompilerParams(
            collective_id=0, has_side_effects=True, vmem_limit_bytes=62 * 1024 * 1024
        ),
    )(
        query_proj, key_proj, value_proj, short_weight, decay_rate, residue,
        skip_gain.reshape(1, channels),
    )


def solution(mesh):
    rows = P(("group", "ctx"), None)
    return jax.shard_map(
        per_device,
        mesh=mesh,
        in_specs=(rows, rows, rows, P(), P(), P(), P()),
        out_specs=rows,
        check_vma=False,
    )
```

```python
import functools

import jax
import jax.numpy as jnp
from jax import lax
from jax.experimental import pallas as pl
from jax.experimental.pallas import tpu as pltpu
from jax.sharding import PartitionSpec as P

MESH = pl.DeviceIdType.MESH
F32 = jnp.float32
BF16 = jnp.bfloat16
LANES = 128
SUBS = 8
WIDE = SUBS * LANES
CHUNK = 8
EDGE = 16


def owning(parts):
    return parts // 4, parts // 2


def tree_sum(terms):
    terms = list(terms)
    while len(terms) > 1:
        half = len(terms) // 2
        rest = terms[2 * half :]
        terms = [terms[i] + terms[i + half] for i in range(half)] + rest
    return terms[0]


def layer_kernel(
    parts, q_hbm, k_hbm, v_hbm, sw_hbm, rate_hbm, res_hbm, skip_hbm, out_ref,
    qbuf, kbuf, vbuf, edge, sw, rate, res, skip,
    qx, kx, vx, tail, halo, sw_t, rate_t, res_t, skip_t,
    a1, a6, a8, a248, a256, w_s, taps, g_s, h_s, y_s, qc_s,
    ends, got, back, inc,
    load_sem, edge_sem, par_sem, halo_sem, direct_sem, send_a, recv_a, send_b, recv_b,
):
    tokens, channels = qbuf.shape
    modes = rate.shape[0]
    halves = channels // WIDE
    first, owners = owning(parts)
    own = modes // owners
    last = parts - 1
    chunks = tokens // CHUNK
    pairs = chunks // 2
    span = tokens + 2
    stage = 4 * EDGE
    stages = tokens // stage
    me = lax.axis_index("ctx")
    owning_here = jnp.logical_and(me >= first, me < first + owners)
    barrier = pltpu.get_barrier_semaphore()

    def row(i, count=1):
        start = i * SUBS
        if not isinstance(start, int):
            start = pl.multiple_of(start, SUBS)
        return pl.ds(start, count * SUBS)

    edge_copies = []
    for m, src in enumerate((q_hbm, k_hbm, v_hbm)):
        edge_copies.append(pltpu.make_async_copy(src.at[pl.ds(tokens - EDGE, EDGE)], edge.at[m], edge_sem.at[m]))
    par_copies = []
    for i, (src, dst) in enumerate(((rate_hbm, rate), (res_hbm, res), (sw_hbm, sw), (skip_hbm, skip))):
        par_copies.append(pltpu.make_async_copy(src, dst, par_sem.at[i]))
    loads = {}
    order = []

    def load(m, src, dst, h, part, first, count):
        at = (pl.ds(first, count), pl.ds(h * WIDE, WIDE))
        loads[m, h, part] = pltpu.make_async_copy(src.at[at], dst.at[at], load_sem.at[len(order)])
        order.append(loads[m, h, part])

    for h in range(halves):
        for part, begin, count in ((0, 0, stage), (1, stage, tokens - stage)):
            load(1, k_hbm, kbuf, h, part, begin, count)
            load(2, v_hbm, vbuf, h, part, begin, count)
    for h in range(halves):
        load(0, q_hbm, qbuf, h, 0, 0, tokens)
    early = [loads[m, 0, part] for part in (0, 1) for m in (1, 2)]
    late = [loads[m, h, part] for h in range(1, halves) for part in (0, 1) for m in (1, 2)]
    late += [loads[0, h, 0] for h in range(halves)]
    for c in par_copies + early[:2] + edge_copies + early[2:]:
        c.start()

    halo[...] = jnp.zeros(halo.shape, F32)
    inc[...] = jnp.zeros(inc.shape, F32)

    def greet(peer, carry=0):
        @pl.when(peer != me)
        def _():
            pl.semaphore_signal(barrier, inc=1, device_id={"ctx": peer}, device_id_type=MESH)

        return carry

    def owns(x):
        return jnp.logical_and(x >= first, x < first + owners)

    lax.fori_loop(jnp.where(owning_here, 0, first), jnp.where(owning_here, parts, first + owners), greet, 0)

    @pl.when(jnp.logical_and(jnp.logical_not(owning_here), jnp.logical_and(me > 0, jnp.logical_not(owns(me - 1)))))
    def _():
        greet(me - 1)

    for dst in (qx, kx, vx):
        for h in range(halves):
            dst[row(h * span, 2), :] = jnp.zeros((2 * SUBS, LANES), F32)

    for c in par_copies:
        c.wait()
    for h in range(halves):
        for s in range(SUBS):
            at = (h * SUBS + s) * LANES
            cols = slice(at, at + LANES)
            rate_t[pl.ds(h * modes * SUBS + s, modes, stride=SUBS), :] = rate[:, cols]
            res_t[pl.ds(h * modes * SUBS + s, modes, stride=SUBS), :] = res[:, cols]
            for m in range(3):
                sw_t[pl.ds((h * 3 + m) * 3 * SUBS + s, 3, stride=SUBS), :] = sw[m, :, cols]
            skip_t[h * SUBS + s : h * SUBS + s + 1, :] = skip[0:1, cols]

    def constants(h, carry):
        zero_lag, sums = [], [[] for _ in range(CHUNK)]
        for n in range(modes):
            at = row(h * modes + n)
            negative = -rate_t[at, :]
            weight = res_t[at, :]
            one = jnp.exp(negative)
            a1[at, :] = one
            a6[at, :] = jnp.exp(negative * float(CHUNK - 2))
            a8[at, :] = jnp.exp(negative * float(CHUNK))
            a248[at, :] = jnp.exp(negative * float(tokens - CHUNK))
            a256[at, :] = jnp.exp(negative * float(tokens))
            zero_lag.append(weight)
            for i in range(CHUNK):
                weight = weight * one
                w_s[row((h * CHUNK + i) * modes + n), :] = weight
                sums[i].append(weight)
        taps[row(h * CHUNK), :] = tree_sum(zero_lag) + skip_t[row(h), :]
        for d in range(1, CHUNK):
            taps[row(h * CHUNK + d), :] = tree_sum(sums[d - 1])
        return carry

    lax.fori_loop(0, halves, constants, 0)
    for c in late:
        c.start()

    for c in edge_copies:
        c.wait()
    for m in range(3):
        for h in range(halves):
            for s in range(SUBS):
                at = (h * SUBS + s) * LANES
                rows = edge[m, :, at : at + LANES].astype(F32)
                tail[pl.ds((m * halves + h) * 2 * SUBS + s, 2, stride=SUBS), :] = rows[EDGE - 2 :, :]

    halo_copy = pltpu.make_async_remote_copy(
        src_ref=tail, dst_ref=halo, send_sem=halo_sem.at[0], recv_sem=halo_sem.at[1],
        device_id={"ctx": lax.rem(me + 1, parts)}, device_id_type=MESH,
    )

    def open_halo():
        to_next = jnp.logical_and(me < last, jnp.logical_not(owns(me + 1)))
        pl.semaphore_wait(barrier, jnp.where(owning_here, last, owners + jnp.where(to_next, 1, 0)))

        @pl.when(me < last)
        def _():
            halo_copy.start()

    def spread(buf, dst, h, at):
        t = at * stage
        source = jnp.minimum(h, halves - 1) if not isinstance(h, int) else min(h, halves - 1)
        for u in range(0, stage, EDGE):
            rows = pl.ds(t + u if isinstance(t, int) else pl.multiple_of(t + u, EDGE), EDGE)
            base = (h * span + 2 + t + u) * SUBS
            for s in range(SUBS):
                lane = source * WIDE + s * LANES
                cols = pl.ds(lane if isinstance(lane, int) else pl.multiple_of(lane, LANES), LANES)
                dst[pl.ds(base + s, EDGE, stride=SUBS), :] = buf[rows, cols].astype(F32)

    def close_halo():
        @pl.when(me > 0)
        def _():
            halo_copy.wait_recv()

    def following(h, at):
        last = at == stages - 1
        return jnp.where(last, h + 1, h), jnp.where(last, 0, at + 1)

    def filtered(ref, m, h, t, count):
        base = h * span + t
        x = [ref[row(base + i), :] for i in range(count + 2)]
        w = [sw_t[row((h * 3 + m) * 3 + lag), :] for lag in range(3)]
        return [w[0] * x[i + 2] + w[1] * x[i + 1] + w[2] * x[i] for i in range(count)]

    def states(h):
        ends[row(h * modes, modes), :] = jnp.zeros((modes * SUBS, LANES), F32)

        def step(at, carry):
            @pl.when(at == 0)
            def _():
                loads[1, h, 1].wait()
                loads[2, h, 1].wait()

            if h + 1 < halves:
                @pl.when(at == stages - 1)
                def _():
                    loads[1, h + 1, 0].wait()
                    loads[2, h + 1, 0].wait()

            total = [ends[row(h * modes + n), :] for n in range(modes)]
            for p in range(stage // (2 * CHUNK)):
                t = at * stage + p * 2 * CHUNK
                kc = filtered(kx, 1, h, t, 2 * CHUNK)
                vc = filtered(vx, 2, h, t, 2 * CHUNK)
                g = [a * b for a, b in zip(kc, vc)]
                for i in range(2 * CHUNK):
                    g_s[row(h * tokens + t + i), :] = g[i]
                for n in range(modes):
                    a = a1[row(h * modes + n), :]
                    factor = a8[row(h * modes + n), :]
                    for c in range(2):
                        local = g[c * CHUNK]
                        for i in range(1, CHUNK):
                            local = a * local + g[c * CHUNK + i]
                        h_s[row((h * chunks + t // CHUNK + c) * modes + n), :] = local
                        total[n] = factor * total[n] + local
            for n in range(modes):
                ends[row(h * modes + n), :] = total[n]
            nh, na = following(h, at)
            spread(kbuf, kx, nh, na)
            spread(vbuf, vx, nh, na)
            if h == 0:
                @pl.when(at == jnp.where(me < 2, stages - 1, 1))
                def _():
                    open_halo()

            if h == 1:
                @pl.when(at == 2)
                def _():
                    close_halo()
                    correct(0)
                    share(0)

            return carry

        lax.fori_loop(0, stages, step, 0)

    def margin(dst, m, h):
        dst[row(h * span, 2), :] = halo[row((m * halves + h) * 2, 2), :]

    def correct(h):
        margin(kx, 1, h)
        margin(vx, 2, h)
        g = [a * b for a, b in zip(filtered(kx, 1, h, 0, 2), filtered(vx, 2, h, 0, 2))]
        change = [g[i] - g_s[row(h * tokens + i), :] for i in range(2)]
        for i in range(2):
            g_s[row(h * tokens + i), :] = g[i]
        for n in range(modes):
            at = row(h * modes + n)
            extra = a6[at, :] * (a1[at, :] * change[0] + change[1])
            first = row(h * chunks * modes + n)
            h_s[first, :] = h_s[first, :] + extra
            ends[at, :] = ends[at, :] + a248[at, :] * extra

    def modes_of(h, owner):
        return row(h * modes + (owner - first) * own, own)

    def sums(h, device):
        return row((h * parts + device) * own, own)

    def send_ends(h, owner):
        return pltpu.make_async_remote_copy(
            src_ref=ends.at[modes_of(h, owner)], dst_ref=got.at[sums(h, me)],
            send_sem=send_a.at[h * owners + owner - first], recv_sem=recv_a.at[h * parts + me],
            device_id={"ctx": owner}, device_id_type=MESH,
        )

    def got_ends(h, p):
        return pltpu.make_async_remote_copy(
            src_ref=ends.at[modes_of(h, first)], dst_ref=got.at[sums(h, p)],
            send_sem=send_a.at[h * owners], recv_sem=recv_a.at[h * parts + p],
            device_id={"ctx": p}, device_id_type=MESH,
        )

    def send_back(h, q):
        return pltpu.make_async_remote_copy(
            src_ref=back.at[sums(h, q)], dst_ref=inc.at[modes_of(h, me)],
            send_sem=send_b.at[h * parts + q], recv_sem=recv_b.at[h * owners + me - first],
            device_id={"ctx": q}, device_id_type=MESH,
        )

    def got_back(h, owner):
        return pltpu.make_async_remote_copy(
            src_ref=back.at[sums(h, 0)], dst_ref=inc.at[modes_of(h, owner)],
            send_sem=send_b.at[h * parts], recv_sem=recv_b.at[h * owners + owner - first],
            device_id={"ctx": owner}, device_id_type=MESH,
        )

    def send_direct(h):
        return pltpu.make_async_remote_copy(
            src_ref=ends.at[row(h * modes, modes)], dst_ref=inc.at[row(h * modes, modes)],
            send_sem=direct_sem.at[2 * h], recv_sem=direct_sem.at[2 * h + 1],
            device_id={"ctx": lax.rem(me + 1, parts)}, device_id_type=MESH,
        )

    def share(h):
        def body(i, carry):
            owner = first + lax.rem(me + i, owners)

            @pl.when(owner != me)
            def _():
                send_ends(h, owner).start()

            return carry

        @pl.when(me < last)
        def _():
            lax.fori_loop(0, owners, body, 0)

        @pl.when(me == 0)
        def _():
            send_direct(h).start()

        @pl.when(owning_here)
        def _():
            got[sums(h, me), :] = ends[modes_of(h, me), :]

    def took(h):
        factor = a256[modes_of(h, me), :]

        def body(p, total):
            @pl.when(p != me)
            def _():
                got_ends(h, p).wait_recv()

            total = factor * total + got[sums(h, p), :]
            q = p + 1

            @pl.when(jnp.logical_and(q != me, q > 1))
            def _():
                back[sums(h, q), :] = total
                send_back(h, q).start()

            @pl.when(q == me)
            def _():
                inc[modes_of(h, me), :] = total

            return total

        lax.fori_loop(0, last, body, jnp.zeros((own * SUBS, LANES), F32))

    def local(h):
        def step(at, carry):
            if h + 1 < halves:
                @pl.when(at == stages - 1)
                def _():
                    loads[0, h + 1, 0].wait()

            tap = [taps[row(h * CHUNK + d), :] for d in range(CHUNK)]
            for c in range(stage // CHUNK):
                t = at * stage + c * CHUNK
                qc = filtered(qx, 0, h, t, CHUNK)
                base = h * tokens + t
                g = [g_s[row(base + i), :] for i in range(CHUNK)]
                for i in range(CHUNK):
                    y_s[row(base + i), :] = tree_sum(tap[d] * g[i - d] for d in range(i + 1))
                    qc_s[row(base + i), :] = qc[i]
            nh, na = following(h, at)
            spread(qbuf, qx, nh, na)
            return carry

        lax.fori_loop(0, stages, step, 0)

    def convert(h, t, values):
        tiles = jnp.swapaxes(jnp.stack(values), 0, 1)
        for s in range(SUBS):
            at = (h * SUBS + s) * LANES
            out_ref[pl.ds(pl.multiple_of(t, 2 * CHUNK), 2 * CHUNK), at : at + LANES] = tiles[s].astype(BF16)

    def finish(h):
        def waits(i, carry):
            owner = first + i

            @pl.when(owner != me)
            def _():
                got_back(h, owner).wait_recv()

            return carry

        @pl.when(me > 1)
        def _():
            lax.fori_loop(0, owners, waits, 0)

        @pl.when(me == 1)
        def _():
            send_direct(h).wait_recv()

        def step(pair, carry):
            t = pair * 2 * CHUNK
            entry = [list(carry), [], []]
            for c in range(2):
                for n in range(modes):
                    entry[c + 1].append(
                        a8[row(h * modes + n), :] * entry[c][n] + h_s[row((h * chunks + pair * 2 + c) * modes + n), :]
                    )
            values = [None] * (2 * CHUNK)
            for i in range(CHUNK):
                w = [w_s[row((h * CHUNK + i) * modes + n), :] for n in range(modes)]
                for c in range(2):
                    at = row(h * tokens + t + c * CHUNK + i)
                    values[c * CHUNK + i] = qc_s[at, :] * (
                        y_s[at, :] + tree_sum(w[n] * entry[c][n] for n in range(modes))
                    )
            convert(h, t, values)
            return tuple(entry[2])

        lax.fori_loop(0, pairs, step, tuple(inc[row(h * modes + n), :] for n in range(modes)))

    loads[1, 0, 0].wait()
    loads[2, 0, 0].wait()
    spread(kbuf, kx, 0, 0)
    spread(vbuf, vx, 0, 0)
    for h in range(halves):
        states(h)
    for h in range(1, halves):
        correct(h)
        share(h)
    loads[0, 0, 0].wait()
    spread(qbuf, qx, 0, 0)
    for h in range(halves):
        margin(qx, 0, h)
    for h in range(halves):
        local(h)

    @pl.when(owning_here)
    def _():
        for h in range(halves):
            took(h)

    for h in range(halves):
        finish(h)

    @pl.when(me < last)
    def _():
        halo_copy.wait_send()

    def sent_ends(i, carry):
        owner = first + i

        @pl.when(owner != me)
        def _():
            for h in range(halves):
                send_ends(h, owner).wait_send()

        return carry

    def sent_back(q, carry):
        @pl.when(q != me)
        def _():
            for h in range(halves):
                send_back(h, q).wait_send()

        return carry

    @pl.when(me < last)
    def _():
        lax.fori_loop(0, owners, sent_ends, 0)

    @pl.when(owning_here)
    def _():
        lax.fori_loop(2, parts, sent_back, 0)

    @pl.when(me == 0)
    def _():
        for h in range(halves):
            send_direct(h).wait_send()


def per_device(query_proj, key_proj, value_proj, short_weight, decay_rate, residue, skip_gain):
    parts = lax.axis_size("ctx")
    tokens, channels = query_proj.shape
    modes = decay_rate.shape[0]
    halves = channels // WIDE
    owners = owning(parts)[1]
    own = modes // owners
    any_space = pl.BlockSpec(memory_space=pltpu.HBM)
    vm = pltpu.VMEM
    dma = pltpu.SemaphoreType.DMA

    def regs(count):
        return vm((count * SUBS, LANES), F32)

    return pl.pallas_call(
        functools.partial(layer_kernel, parts),
        out_shape=pltpu.VMEM((tokens, channels), BF16),
        in_specs=[any_space] * 7,
        out_specs=pl.BlockSpec(memory_space=pltpu.VMEM),
        scratch_shapes=[
            vm((tokens, channels), BF16),
            vm((tokens, channels), BF16),
            vm((tokens, channels), BF16),
            vm((3, EDGE, channels), BF16),
            vm(short_weight.shape, F32),
            vm(decay_rate.shape, F32),
            vm(residue.shape, F32),
            vm((1, channels), F32),
            regs((halves + 1) * (tokens + 2)),
            regs((halves + 1) * (tokens + 2)),
            regs((halves + 1) * (tokens + 2)),
            regs(3 * halves * 2),
            regs(3 * halves * 2),
            regs(halves * 9),
            regs(halves * modes),
            regs(halves * modes),
            regs(halves),
            regs(halves * modes),
            regs(halves * modes),
            regs(halves * modes),
            regs(halves * modes),
            regs(halves * modes),
            regs(halves * CHUNK * modes),
            regs(halves * CHUNK),
            regs(halves * tokens),
            regs(halves * tokens // CHUNK * modes),
            regs(halves * tokens),
            regs(halves * tokens),
            regs(halves * modes),
            regs(halves * parts * own),
            regs(halves * parts * own),
            regs(halves * modes),
            dma((5 * halves,)),
            dma((3,)),
            dma((4,)),
            dma((2,)),
            dma((2 * halves,)),
            dma((halves * owners,)),
            dma((halves * parts,)),
            dma((halves * parts,)),
            dma((halves * owners,)),
        ],
        compiler_params=pltpu.CompilerParams(
            collective_id=0, has_side_effects=True, vmem_limit_bytes=62 * 1024 * 1024
        ),
    )(
        query_proj, key_proj, value_proj, short_weight, decay_rate, residue,
        skip_gain.reshape(1, channels),
    )


def solution(mesh):
    rows = P(("group", "ctx"), None)
    return jax.shard_map(
        per_device,
        mesh=mesh,
        in_specs=(rows, rows, rows, P(), P(), P(), P()),
        out_specs=rows,
        check_vma=False,
    )
```

```python
import functools

import jax
import jax.numpy as jnp
from jax import lax
from jax.experimental import pallas as pl
from jax.experimental.pallas import tpu as pltpu
from jax.sharding import PartitionSpec as P

MESH = pl.DeviceIdType.MESH
F32 = jnp.float32
BF16 = jnp.bfloat16
LANES = 128
SUBS = 8
WIDE = SUBS * LANES
CHUNK = 8
EDGE = 16


def owning(parts):
    return parts // 4, parts // 2


def tree_sum(terms):
    terms = list(terms)
    while len(terms) > 1:
        half = len(terms) // 2
        rest = terms[2 * half :]
        terms = [terms[i] + terms[i + half] for i in range(half)] + rest
    return terms[0]


def chain_sum(terms, lanes):
    totals = []
    for i, term in enumerate(terms):
        if i < lanes:
            totals.append(term)
        else:
            totals[i % lanes] = totals[i % lanes] + term
    return tree_sum(totals)


def layer_kernel(
    parts, q_hbm, k_hbm, v_hbm, sw_hbm, rate_hbm, res_hbm, skip_hbm, out_ref,
    qbuf, kbuf, vbuf, edge, sw, rate, res, skip,
    qx, kx, vx, tail, halo, sw_t, rate_t, res_t, skip_t,
    a1, a6, a8, a248, a256, w_s, taps, g_s, h_s, y_s, qc_s,
    ends, got, back, inc,
    load_sem, edge_sem, par_sem, halo_sem, direct_sem, send_a, recv_a, send_b, recv_b,
):
    tokens, channels = qbuf.shape
    modes = rate.shape[0]
    halves = channels // WIDE
    first, owners = owning(parts)
    own = modes // owners
    last = parts - 1
    chunks = tokens // CHUNK
    pairs = chunks // 2
    span = tokens + 2
    stage = 4 * EDGE
    stages = tokens // stage
    me = lax.axis_index("ctx")
    owning_here = jnp.logical_and(me >= first, me < first + owners)
    barrier = pltpu.get_barrier_semaphore()

    def row(i, count=1):
        start = i * SUBS
        if not isinstance(start, int):
            start = pl.multiple_of(start, SUBS)
        return pl.ds(start, count * SUBS)

    edge_copies = []
    for m, src in enumerate((q_hbm, k_hbm, v_hbm)):
        edge_copies.append(pltpu.make_async_copy(src.at[pl.ds(tokens - EDGE, EDGE)], edge.at[m], edge_sem.at[m]))
    par_copies = []
    for i, (src, dst) in enumerate(((rate_hbm, rate), (res_hbm, res), (sw_hbm, sw), (skip_hbm, skip))):
        par_copies.append(pltpu.make_async_copy(src, dst, par_sem.at[i]))
    loads = {}
    order = []

    def load(m, src, dst, h, part, first, count):
        at = (pl.ds(first, count), pl.ds(h * WIDE, WIDE))
        loads[m, h, part] = pltpu.make_async_copy(src.at[at], dst.at[at], load_sem.at[len(order)])
        order.append(loads[m, h, part])

    for h in range(halves):
        for part, begin, count in ((0, 0, stage), (1, stage, tokens - stage)):
            load(1, k_hbm, kbuf, h, part, begin, count)
            load(2, v_hbm, vbuf, h, part, begin, count)
    for h in range(halves):
        load(0, q_hbm, qbuf, h, 0, 0, tokens)
    early = [loads[m, 0, part] for part in (0, 1) for m in (1, 2)]
    late = [loads[m, h, part] for h in range(1, halves) for part in (0, 1) for m in (1, 2)]
    late += [loads[0, h, 0] for h in range(halves)]
    for c in par_copies + early[:2] + edge_copies + early[2:]:
        c.start()

    halo[...] = jnp.zeros(halo.shape, F32)
    inc[...] = jnp.zeros(inc.shape, F32)

    def greet(peer, carry=0):
        @pl.when(peer != me)
        def _():
            pl.semaphore_signal(barrier, inc=1, device_id={"ctx": peer}, device_id_type=MESH)

        return carry

    def owns(x):
        return jnp.logical_and(x >= first, x < first + owners)

    lax.fori_loop(jnp.where(owning_here, 0, first), jnp.where(owning_here, parts, first + owners), greet, 0)

    @pl.when(jnp.logical_and(jnp.logical_not(owning_here), jnp.logical_and(me > 0, jnp.logical_not(owns(me - 1)))))
    def _():
        greet(me - 1)

    for dst in (qx, kx, vx):
        for h in range(halves):
            dst[row(h * span, 2), :] = jnp.zeros((2 * SUBS, LANES), F32)

    for c in par_copies:
        c.wait()
    for h in range(halves):
        for s in range(SUBS):
            at = (h * SUBS + s) * LANES
            cols = slice(at, at + LANES)
            rate_t[pl.ds(h * modes * SUBS + s, modes, stride=SUBS), :] = rate[:, cols]
            res_t[pl.ds(h * modes * SUBS + s, modes, stride=SUBS), :] = res[:, cols]
            for m in range(3):
                sw_t[pl.ds((h * 3 + m) * 3 * SUBS + s, 3, stride=SUBS), :] = sw[m, :, cols]
            skip_t[h * SUBS + s : h * SUBS + s + 1, :] = skip[0:1, cols]

    def constants(h, carry):
        zero_lag, sums = [], [[] for _ in range(CHUNK)]
        for n in range(modes):
            at = row(h * modes + n)
            negative = -rate_t[at, :]
            weight = res_t[at, :]
            one = jnp.exp(negative)
            a1[at, :] = one
            a6[at, :] = jnp.exp(negative * float(CHUNK - 2))
            a8[at, :] = jnp.exp(negative * float(CHUNK))
            a248[at, :] = jnp.exp(negative * float(tokens - CHUNK))
            a256[at, :] = jnp.exp(negative * float(tokens))
            zero_lag.append(weight)
            for i in range(CHUNK):
                weight = weight * one
                w_s[row((h * CHUNK + i) * modes + n), :] = weight
                sums[i].append(weight)
        taps[row(h * CHUNK), :] = tree_sum(zero_lag) + skip_t[row(h), :]
        for d in range(1, CHUNK):
            taps[row(h * CHUNK + d), :] = tree_sum(sums[d - 1])
        return carry

    lax.fori_loop(0, halves, constants, 0)
    for c in late:
        c.start()

    for c in edge_copies:
        c.wait()
    for m in range(3):
        for h in range(halves):
            for s in range(SUBS):
                at = (h * SUBS + s) * LANES
                rows = edge[m, :, at : at + LANES].astype(F32)
                tail[pl.ds((m * halves + h) * 2 * SUBS + s, 2, stride=SUBS), :] = rows[EDGE - 2 :, :]

    halo_copy = pltpu.make_async_remote_copy(
        src_ref=tail, dst_ref=halo, send_sem=halo_sem.at[0], recv_sem=halo_sem.at[1],
        device_id={"ctx": lax.rem(me + 1, parts)}, device_id_type=MESH,
    )

    def open_halo():
        to_next = jnp.logical_and(me < last, jnp.logical_not(owns(me + 1)))
        pl.semaphore_wait(barrier, jnp.where(owning_here, last, owners + jnp.where(to_next, 1, 0)))

        @pl.when(me < last)
        def _():
            halo_copy.start()

    def spread(buf, dst, h, at):
        t = at * stage
        source = jnp.minimum(h, halves - 1) if not isinstance(h, int) else min(h, halves - 1)
        for u in range(0, stage, EDGE):
            rows = pl.ds(t + u if isinstance(t, int) else pl.multiple_of(t + u, EDGE), EDGE)
            base = (h * span + 2 + t + u) * SUBS
            for s in range(SUBS):
                lane = source * WIDE + s * LANES
                cols = pl.ds(lane if isinstance(lane, int) else pl.multiple_of(lane, LANES), LANES)
                dst[pl.ds(base + s, EDGE, stride=SUBS), :] = buf[rows, cols].astype(F32)

    def close_halo():
        @pl.when(me > 0)
        def _():
            halo_copy.wait_recv()

    def following(h, at):
        last = at == stages - 1
        return jnp.where(last, h + 1, h), jnp.where(last, 0, at + 1)

    def filtered(ref, m, h, t, count):
        base = h * span + t
        x = [ref[row(base + i), :] for i in range(count + 2)]
        w = [sw_t[row((h * 3 + m) * 3 + lag), :] for lag in range(3)]
        return [w[0] * x[i + 2] + w[1] * x[i + 1] + w[2] * x[i] for i in range(count)]

    def states(h):
        ends[row(h * modes, modes), :] = jnp.zeros((modes * SUBS, LANES), F32)

        def step(at, carry):
            @pl.when(at == 0)
            def _():
                loads[1, h, 1].wait()
                loads[2, h, 1].wait()

            if h + 1 < halves:
                @pl.when(at == stages - 1)
                def _():
                    loads[1, h + 1, 0].wait()
                    loads[2, h + 1, 0].wait()

            total = [ends[row(h * modes + n), :] for n in range(modes)]
            for p in range(stage // (2 * CHUNK)):
                t = at * stage + p * 2 * CHUNK
                kc = filtered(kx, 1, h, t, 2 * CHUNK)
                vc = filtered(vx, 2, h, t, 2 * CHUNK)
                g = [a * b for a, b in zip(kc, vc)]
                for i in range(2 * CHUNK):
                    g_s[row(h * tokens + t + i), :] = g[i]
                for n in range(modes):
                    a = a1[row(h * modes + n), :]
                    factor = a8[row(h * modes + n), :]
                    for c in range(2):
                        local = g[c * CHUNK]
                        for i in range(1, CHUNK):
                            local = a * local + g[c * CHUNK + i]
                        h_s[row((h * chunks + t // CHUNK + c) * modes + n), :] = local
                        total[n] = factor * total[n] + local
            for n in range(modes):
                ends[row(h * modes + n), :] = total[n]
            nh, na = following(h, at)
            spread(kbuf, kx, nh, na)
            spread(vbuf, vx, nh, na)
            if h == 0:
                @pl.when(at == jnp.where(me < 2, stages - 1, jnp.where(me < 6, 0, -1)))
                def _():
                    open_halo()

            if h == 1:
                @pl.when(at == jnp.where(me < 6, 1, 0))
                def _():
                    close_halo()
                    correct(0)
                    share(0)

            return carry

        lax.fori_loop(0, stages, step, 0)

    def margin(dst, m, h):
        dst[row(h * span, 2), :] = halo[row((m * halves + h) * 2, 2), :]

    def correct(h):
        margin(kx, 1, h)
        margin(vx, 2, h)
        g = [a * b for a, b in zip(filtered(kx, 1, h, 0, 2), filtered(vx, 2, h, 0, 2))]
        change = [g[i] - g_s[row(h * tokens + i), :] for i in range(2)]
        for i in range(2):
            g_s[row(h * tokens + i), :] = g[i]
        for n in range(modes):
            at = row(h * modes + n)
            extra = a6[at, :] * (a1[at, :] * change[0] + change[1])
            first = row(h * chunks * modes + n)
            h_s[first, :] = h_s[first, :] + extra
            ends[at, :] = ends[at, :] + a248[at, :] * extra

    def modes_of(h, owner):
        return row(h * modes + (owner - first) * own, own)

    def sums(h, device):
        return row((h * parts + device) * own, own)

    def send_ends(h, owner):
        return pltpu.make_async_remote_copy(
            src_ref=ends.at[modes_of(h, owner)], dst_ref=got.at[sums(h, me)],
            send_sem=send_a.at[h * owners + owner - first], recv_sem=recv_a.at[h * parts + me],
            device_id={"ctx": owner}, device_id_type=MESH,
        )

    def got_ends(h, p):
        return pltpu.make_async_remote_copy(
            src_ref=ends.at[modes_of(h, first)], dst_ref=got.at[sums(h, p)],
            send_sem=send_a.at[h * owners], recv_sem=recv_a.at[h * parts + p],
            device_id={"ctx": p}, device_id_type=MESH,
        )

    def send_back(h, q):
        return pltpu.make_async_remote_copy(
            src_ref=back.at[sums(h, q)], dst_ref=inc.at[modes_of(h, me)],
            send_sem=send_b.at[h * parts + q], recv_sem=recv_b.at[h * owners + me - first],
            device_id={"ctx": q}, device_id_type=MESH,
        )

    def got_back(h, owner):
        return pltpu.make_async_remote_copy(
            src_ref=back.at[sums(h, 0)], dst_ref=inc.at[modes_of(h, owner)],
            send_sem=send_b.at[h * parts], recv_sem=recv_b.at[h * owners + owner - first],
            device_id={"ctx": owner}, device_id_type=MESH,
        )

    def send_direct(h):
        return pltpu.make_async_remote_copy(
            src_ref=ends.at[row(h * modes, modes)], dst_ref=inc.at[row(h * modes, modes)],
            send_sem=direct_sem.at[2 * h], recv_sem=direct_sem.at[2 * h + 1],
            device_id={"ctx": lax.rem(me + 1, parts)}, device_id_type=MESH,
        )

    def share(h):
        def body(i, carry):
            owner = first + lax.rem(me + i, owners)

            @pl.when(owner != me)
            def _():
                send_ends(h, owner).start()

            return carry

        @pl.when(me < last)
        def _():
            lax.fori_loop(0, owners, body, 0)

        @pl.when(me == 0)
        def _():
            send_direct(h).start()

        @pl.when(owning_here)
        def _():
            got[sums(h, me), :] = ends[modes_of(h, me), :]

    def took(h):
        factor = a256[modes_of(h, me), :]

        def body(p, total):
            @pl.when(p != me)
            def _():
                got_ends(h, p).wait_recv()

            total = factor * total + got[sums(h, p), :]
            q = p + 1

            @pl.when(jnp.logical_and(q != me, q > 1))
            def _():
                back[sums(h, q), :] = total
                send_back(h, q).start()

            @pl.when(q == me)
            def _():
                inc[modes_of(h, me), :] = total

            return total

        lax.fori_loop(0, last, body, jnp.zeros((own * SUBS, LANES), F32))

    def local(h):
        def step(at, carry):
            if h + 1 < halves:
                @pl.when(at == stages - 1)
                def _():
                    loads[0, h + 1, 0].wait()

            tap = [taps[row(h * CHUNK + d), :] for d in range(CHUNK)]
            for c in range(stage // CHUNK):
                t = at * stage + c * CHUNK
                qc = filtered(qx, 0, h, t, CHUNK)
                base = h * tokens + t
                g = [g_s[row(base + i), :] for i in range(CHUNK)]
                for i in range(CHUNK):
                    y_s[row(base + i), :] = tree_sum(tap[d] * g[i - d] for d in range(i + 1))
                    qc_s[row(base + i), :] = qc[i]
            nh, na = following(h, at)
            spread(qbuf, qx, nh, na)
            return carry

        lax.fori_loop(0, stages, step, 0)

    def convert(h, t, values):
        tiles = jnp.swapaxes(jnp.stack(values), 0, 1)
        for s in range(SUBS):
            at = (h * SUBS + s) * LANES
            out_ref[pl.ds(pl.multiple_of(t, 2 * CHUNK), 2 * CHUNK), at : at + LANES] = tiles[s].astype(BF16)

    def finish(h):
        def waits(i, carry):
            owner = first + i

            @pl.when(owner != me)
            def _():
                got_back(h, owner).wait_recv()

            return carry

        @pl.when(me > 1)
        def _():
            lax.fori_loop(0, owners, waits, 0)

        @pl.when(me == 1)
        def _():
            send_direct(h).wait_recv()

        def step(at, carry):
            entry = list(carry)
            for p in range(4):
                t = (at * 4 + p) * 2 * CHUNK
                values = []
                for c in range(2):
                    for i in range(CHUNK):
                        here = row(h * tokens + t + c * CHUNK + i)
                        total = chain_sum((w_s[row((h * CHUNK + i) * modes + n), :] * entry[n] for n in range(modes)), 2)
                        values.append(qc_s[here, :] * (y_s[here, :] + total))
                    entry = [
                        a8[row(h * modes + n), :] * entry[n]
                        + h_s[row((h * chunks + (at * 4 + p) * 2 + c) * modes + n), :]
                        for n in range(modes)
                    ]
                convert(h, t, values)
            return tuple(entry)

        lax.fori_loop(0, pairs // 4, step, tuple(inc[row(h * modes + n), :] for n in range(modes)))

    loads[1, 0, 0].wait()
    loads[2, 0, 0].wait()
    spread(kbuf, kx, 0, 0)
    spread(vbuf, vx, 0, 0)
    @pl.when(me >= 6)
    def _():
        open_halo()

    for h in range(halves):
        states(h)
    for h in range(1, halves):
        correct(h)
        share(h)
    @pl.when(owning_here)
    def _():
        for h in range(halves):
            took(h)

    loads[0, 0, 0].wait()
    spread(qbuf, qx, 0, 0)
    for h in range(halves):
        margin(qx, 0, h)
    for h in range(halves):
        local(h)

    for h in range(halves):
        finish(h)

    @pl.when(me < last)
    def _():
        halo_copy.wait_send()

    def sent_ends(i, carry):
        owner = first + i

        @pl.when(owner != me)
        def _():
            for h in range(halves):
                send_ends(h, owner).wait_send()

        return carry

    def sent_back(q, carry):
        @pl.when(q != me)
        def _():
            for h in range(halves):
                send_back(h, q).wait_send()

        return carry

    @pl.when(me < last)
    def _():
        lax.fori_loop(0, owners, sent_ends, 0)

    @pl.when(owning_here)
    def _():
        lax.fori_loop(2, parts, sent_back, 0)

    @pl.when(me == 0)
    def _():
        for h in range(halves):
            send_direct(h).wait_send()


def per_device(query_proj, key_proj, value_proj, short_weight, decay_rate, residue, skip_gain):
    parts = lax.axis_size("ctx")
    tokens, channels = query_proj.shape
    modes = decay_rate.shape[0]
    halves = channels // WIDE
    owners = owning(parts)[1]
    own = modes // owners
    any_space = pl.BlockSpec(memory_space=pltpu.HBM)
    vm = pltpu.VMEM
    dma = pltpu.SemaphoreType.DMA

    def regs(count):
        return vm((count * SUBS, LANES), F32)

    return pl.pallas_call(
        functools.partial(layer_kernel, parts),
        out_shape=pltpu.VMEM((tokens, channels), BF16),
        in_specs=[any_space] * 7,
        out_specs=pl.BlockSpec(memory_space=pltpu.VMEM),
        scratch_shapes=[
            vm((tokens, channels), BF16),
            vm((tokens, channels), BF16),
            vm((tokens, channels), BF16),
            vm((3, EDGE, channels), BF16),
            vm(short_weight.shape, F32),
            vm(decay_rate.shape, F32),
            vm(residue.shape, F32),
            vm((1, channels), F32),
            regs((halves + 1) * (tokens + 2)),
            regs((halves + 1) * (tokens + 2)),
            regs((halves + 1) * (tokens + 2)),
            regs(3 * halves * 2),
            regs(3 * halves * 2),
            regs(halves * 9),
            regs(halves * modes),
            regs(halves * modes),
            regs(halves),
            regs(halves * modes),
            regs(halves * modes),
            regs(halves * modes),
            regs(halves * modes),
            regs(halves * modes),
            regs(halves * CHUNK * modes),
            regs(halves * CHUNK),
            regs(halves * tokens),
            regs(halves * tokens // CHUNK * modes),
            regs(halves * tokens),
            regs(halves * tokens),
            regs(halves * modes),
            regs(halves * parts * own),
            regs(halves * parts * own),
            regs(halves * modes),
            dma((5 * halves,)),
            dma((3,)),
            dma((4,)),
            dma((2,)),
            dma((2 * halves,)),
            dma((halves * owners,)),
            dma((halves * parts,)),
            dma((halves * parts,)),
            dma((halves * owners,)),
        ],
        compiler_params=pltpu.CompilerParams(
            collective_id=0, has_side_effects=True, vmem_limit_bytes=62 * 1024 * 1024
        ),
    )(
        query_proj, key_proj, value_proj, short_weight, decay_rate, residue,
        skip_gain.reshape(1, channels),
    )


def solution(mesh):
    rows = P(("group", "ctx"), None)
    return jax.shard_map(
        per_device,
        mesh=mesh,
        in_specs=(rows, rows, rows, P(), P(), P(), P()),
        out_specs=rows,
        check_vma=False,
    )
```

```python
import functools

import jax
import jax.numpy as jnp
from jax import lax
from jax.experimental import pallas as pl
from jax.experimental.pallas import tpu as pltpu
from jax.sharding import PartitionSpec as P

MESH = pl.DeviceIdType.MESH
F32 = jnp.float32
BF16 = jnp.bfloat16
LANES = 128
SUBS = 8
WIDE = SUBS * LANES
CHUNK = 8
EDGE = 16


def owning(parts):
    return parts // 4, parts // 2


def tree_sum(terms):
    terms = list(terms)
    while len(terms) > 1:
        half = len(terms) // 2
        rest = terms[2 * half :]
        terms = [terms[i] + terms[i + half] for i in range(half)] + rest
    return terms[0]


def chain_sum(terms, lanes):
    totals = []
    for i, term in enumerate(terms):
        if i < lanes:
            totals.append(term)
        else:
            totals[i % lanes] = totals[i % lanes] + term
    return tree_sum(totals)


def layer_kernel(
    parts, q_hbm, k_hbm, v_hbm, sw_hbm, rate_hbm, res_hbm, skip_hbm, out_ref,
    qbuf, kbuf, vbuf, edge, sw, rate, res, skip,
    qx, kx, vx, tail, halo, sw_t, rate_t, res_t, skip_t,
    a1, a6, a8, a248, a256, w_s, taps, g_s, h_s, y_s, qc_s,
    ends, got, back, inc,
    load_sem, edge_sem, par_sem, halo_sem, direct_sem, send_a, recv_a, send_b, recv_b,
):
    tokens, channels = qbuf.shape
    modes = rate.shape[0]
    halves = channels // WIDE
    first, owners = owning(parts)
    own = modes // owners
    last = parts - 1
    chunks = tokens // CHUNK
    pairs = chunks // 2
    span = tokens + 2
    stage = 4 * EDGE
    stages = tokens // stage
    me = lax.axis_index("ctx")
    owning_here = jnp.logical_and(me >= first, me < first + owners)
    barrier = pltpu.get_barrier_semaphore()

    def row(i, count=1):
        start = i * SUBS
        if not isinstance(start, int):
            start = pl.multiple_of(start, SUBS)
        return pl.ds(start, count * SUBS)

    edge_copies = []
    for m, src in enumerate((q_hbm, k_hbm, v_hbm)):
        edge_copies.append(pltpu.make_async_copy(src.at[pl.ds(tokens - EDGE, EDGE)], edge.at[m], edge_sem.at[m]))
    par_copies = []
    for i, (src, dst) in enumerate(((rate_hbm, rate), (res_hbm, res), (sw_hbm, sw), (skip_hbm, skip))):
        par_copies.append(pltpu.make_async_copy(src, dst, par_sem.at[i]))
    loads = {}
    order = []

    def load(m, src, dst, h, part, first, count):
        at = (pl.ds(first, count), pl.ds(h * WIDE, WIDE))
        loads[m, h, part] = pltpu.make_async_copy(src.at[at], dst.at[at], load_sem.at[len(order)])
        order.append(loads[m, h, part])

    for h in range(halves):
        for part, begin, count in ((0, 0, stage), (1, stage, tokens - stage)):
            load(1, k_hbm, kbuf, h, part, begin, count)
            load(2, v_hbm, vbuf, h, part, begin, count)
    for h in range(halves):
        load(0, q_hbm, qbuf, h, 0, 0, tokens)
    early = [loads[m, 0, part] for part in (0, 1) for m in (1, 2)]
    late = [loads[m, h, part] for h in range(1, halves) for part in (0, 1) for m in (1, 2)]
    late += [loads[0, h, 0] for h in range(halves)]
    for c in par_copies + early[:2] + edge_copies + early[2:]:
        c.start()

    halo[...] = jnp.zeros(halo.shape, F32)
    inc[...] = jnp.zeros(inc.shape, F32)

    def greet(peer, carry=0):
        @pl.when(peer != me)
        def _():
            pl.semaphore_signal(barrier, inc=1, device_id={"ctx": peer}, device_id_type=MESH)

        return carry

    def owns(x):
        return jnp.logical_and(x >= first, x < first + owners)

    lax.fori_loop(jnp.where(owning_here, 0, first), jnp.where(owning_here, parts, first + owners), greet, 0)

    @pl.when(jnp.logical_and(jnp.logical_not(owning_here), jnp.logical_and(me > 0, jnp.logical_not(owns(me - 1)))))
    def _():
        greet(me - 1)

    for dst in (qx, kx, vx):
        for h in range(halves):
            dst[row(h * span, 2), :] = jnp.zeros((2 * SUBS, LANES), F32)

    for c in par_copies:
        c.wait()
    for h in range(halves):
        for s in range(SUBS):
            at = (h * SUBS + s) * LANES
            cols = slice(at, at + LANES)
            rate_t[pl.ds(h * modes * SUBS + s, modes, stride=SUBS), :] = rate[:, cols]
            res_t[pl.ds(h * modes * SUBS + s, modes, stride=SUBS), :] = res[:, cols]
            for m in range(3):
                sw_t[pl.ds((h * 3 + m) * 3 * SUBS + s, 3, stride=SUBS), :] = sw[m, :, cols]
            skip_t[h * SUBS + s : h * SUBS + s + 1, :] = skip[0:1, cols]

    def constants(h, carry):
        zero_lag, sums = [], [[] for _ in range(CHUNK)]
        for n in range(modes):
            at = row(h * modes + n)
            negative = -rate_t[at, :]
            weight = res_t[at, :]
            one = jnp.exp(negative)
            a1[at, :] = one
            a6[at, :] = jnp.exp(negative * float(CHUNK - 2))
            a8[at, :] = jnp.exp(negative * float(CHUNK))
            a248[at, :] = jnp.exp(negative * float(tokens - CHUNK))
            a256[at, :] = jnp.exp(negative * float(tokens))
            zero_lag.append(weight)
            for i in range(CHUNK):
                weight = weight * one
                w_s[row((h * CHUNK + i) * modes + n), :] = weight
                sums[i].append(weight)
        taps[row(h * CHUNK), :] = tree_sum(zero_lag) + skip_t[row(h), :]
        for d in range(1, CHUNK):
            taps[row(h * CHUNK + d), :] = tree_sum(sums[d - 1])
        return carry

    lax.fori_loop(0, halves, constants, 0)
    for c in late:
        c.start()

    for c in edge_copies:
        c.wait()
    for m in range(3):
        for h in range(halves):
            for s in range(SUBS):
                at = (h * SUBS + s) * LANES
                rows = edge[m, :, at : at + LANES].astype(F32)
                tail[pl.ds((m * halves + h) * 2 * SUBS + s, 2, stride=SUBS), :] = rows[EDGE - 2 :, :]

    halo_copy = pltpu.make_async_remote_copy(
        src_ref=tail.at[row(0, 3 * halves * 2)], dst_ref=halo, send_sem=halo_sem.at[0], recv_sem=halo_sem.at[1],
        device_id={"ctx": lax.rem(me + 1, parts)}, device_id_type=MESH,
    )

    def open_halo():
        to_next = jnp.logical_and(me < last, jnp.logical_not(owns(me + 1)))
        pl.semaphore_wait(barrier, jnp.where(owning_here, last, owners + jnp.where(to_next, 1, 0)))

        @pl.when(me < last)
        def _():
            halo_copy.start()

    def spread(buf, dst, h, at):
        t = at * stage
        source = jnp.minimum(h, halves - 1) if not isinstance(h, int) else min(h, halves - 1)
        for u in range(0, stage, EDGE):
            rows = pl.ds(t + u if isinstance(t, int) else pl.multiple_of(t + u, EDGE), EDGE)
            base = (h * span + 2 + t + u) * SUBS
            for s in range(SUBS):
                lane = source * WIDE + s * LANES
                cols = pl.ds(lane if isinstance(lane, int) else pl.multiple_of(lane, LANES), LANES)
                dst[pl.ds(base + s, EDGE, stride=SUBS), :] = buf[rows, cols].astype(F32)

    def close_halo():
        @pl.when(me > 0)
        def _():
            halo_copy.wait_recv()

    def following(h, at):
        last = at == stages - 1
        return jnp.where(last, h + 1, h), jnp.where(last, 0, at + 1)

    def filtered(ref, m, h, t, count):
        base = h * span + t
        x = [ref[row(base + i), :] for i in range(count + 2)]
        w = [sw_t[row((h * 3 + m) * 3 + lag), :] for lag in range(3)]
        return [w[0] * x[i + 2] + w[1] * x[i + 1] + w[2] * x[i] for i in range(count)]

    def states(h):
        ends[row(h * modes, modes), :] = jnp.zeros((modes * SUBS, LANES), F32)

        def step(at, carry):
            @pl.when(at == 0)
            def _():
                loads[1, h, 1].wait()
                loads[2, h, 1].wait()

            if h + 1 < halves:
                @pl.when(at == stages - 1)
                def _():
                    loads[1, h + 1, 0].wait()
                    loads[2, h + 1, 0].wait()

            total = [ends[row(h * modes + n), :] for n in range(modes)]
            for p in range(stage // (2 * CHUNK)):
                t = at * stage + p * 2 * CHUNK
                kc = filtered(kx, 1, h, t, 2 * CHUNK)
                vc = filtered(vx, 2, h, t, 2 * CHUNK)
                g = [a * b for a, b in zip(kc, vc)]
                for i in range(2 * CHUNK):
                    g_s[row(h * tokens + t + i), :] = g[i]
                for n in range(modes):
                    a = a1[row(h * modes + n), :]
                    factor = a8[row(h * modes + n), :]
                    for c in range(2):
                        local = g[c * CHUNK]
                        for i in range(1, CHUNK):
                            local = a * local + g[c * CHUNK + i]
                        h_s[row((h * chunks + t // CHUNK + c) * modes + n), :] = local
                        total[n] = factor * total[n] + local
            for n in range(modes):
                ends[row(h * modes + n), :] = total[n]
            nh, na = following(h, at)
            spread(kbuf, kx, nh, na)
            spread(vbuf, vx, nh, na)
            if h == 0:
                @pl.when(at == jnp.where(me < 2, stages - 1, jnp.where(me < 6, 0, -1)))
                def _():
                    open_halo()

            if h == 1:
                @pl.when(at == jnp.where(me < 6, 1, 0))
                def _():
                    close_halo()
                    correct(0)
                    share(0)

            return carry

        lax.fori_loop(0, stages, step, 0)

    def margin(dst, m, h):
        dst[row(h * span, 2), :] = halo[row((m * halves + h) * 2, 2), :]

    def correct(h):
        margin(kx, 1, h)
        margin(vx, 2, h)
        g = [a * b for a, b in zip(filtered(kx, 1, h, 0, 2), filtered(vx, 2, h, 0, 2))]
        change = [g[i] - g_s[row(h * tokens + i), :] for i in range(2)]
        for i in range(2):
            g_s[row(h * tokens + i), :] = g[i]
        for n in range(modes):
            at = row(h * modes + n)
            extra = a6[at, :] * (a1[at, :] * change[0] + change[1])
            first = row(h * chunks * modes + n)
            h_s[first, :] = h_s[first, :] + extra
            ends[at, :] = ends[at, :] + a248[at, :] * extra

    def modes_of(h, owner):
        return row(h * modes + (owner - first) * own, own)

    def sums(h, device):
        return row((h * parts + device) * own, own)

    def send_ends(h, owner):
        return pltpu.make_async_remote_copy(
            src_ref=ends.at[modes_of(h, owner)], dst_ref=got.at[sums(h, me)],
            send_sem=send_a.at[h * owners + owner - first], recv_sem=recv_a.at[h * parts + me],
            device_id={"ctx": owner}, device_id_type=MESH,
        )

    def got_ends(h, p):
        return pltpu.make_async_remote_copy(
            src_ref=ends.at[modes_of(h, first)], dst_ref=got.at[sums(h, p)],
            send_sem=send_a.at[h * owners], recv_sem=recv_a.at[h * parts + p],
            device_id={"ctx": p}, device_id_type=MESH,
        )

    def send_back(h, q):
        return pltpu.make_async_remote_copy(
            src_ref=back.at[sums(h, q)], dst_ref=inc.at[modes_of(h, me)],
            send_sem=send_b.at[h * parts + q], recv_sem=recv_b.at[h * owners + me - first],
            device_id={"ctx": q}, device_id_type=MESH,
        )

    def got_back(h, owner):
        return pltpu.make_async_remote_copy(
            src_ref=back.at[sums(h, 0)], dst_ref=inc.at[modes_of(h, owner)],
            send_sem=send_b.at[h * parts], recv_sem=recv_b.at[h * owners + owner - first],
            device_id={"ctx": owner}, device_id_type=MESH,
        )

    def send_direct(h):
        return pltpu.make_async_remote_copy(
            src_ref=ends.at[row(h * modes, modes)], dst_ref=inc.at[row(h * modes, modes)],
            send_sem=direct_sem.at[2 * h], recv_sem=direct_sem.at[2 * h + 1],
            device_id={"ctx": lax.rem(me + 1, parts)}, device_id_type=MESH,
        )

    def share(h):
        def body(i, carry):
            owner = first + lax.rem(me + i, owners)

            @pl.when(owner != me)
            def _():
                send_ends(h, owner).start()

            return carry

        @pl.when(me < last)
        def _():
            lax.fori_loop(0, owners, body, 0)

        @pl.when(me == 0)
        def _():
            send_direct(h).start()

        @pl.when(owning_here)
        def _():
            got[sums(h, me), :] = ends[modes_of(h, me), :]

    def took(h):
        factor = a256[modes_of(h, me), :]

        def body(p, total):
            @pl.when(p != me)
            def _():
                got_ends(h, p).wait_recv()

            total = factor * total + got[sums(h, p), :]
            q = p + 1

            @pl.when(jnp.logical_and(q != me, q > 1))
            def _():
                back[sums(h, q), :] = total
                send_back(h, q).start()

            @pl.when(q == me)
            def _():
                inc[modes_of(h, me), :] = total

            return total

        lax.fori_loop(0, last, body, jnp.zeros((own * SUBS, LANES), F32))

    def local(h):
        def step(at, carry):
            if h + 1 < halves:
                @pl.when(at == stages - 1)
                def _():
                    loads[0, h + 1, 0].wait()

            tap = [taps[row(h * CHUNK + d), :] for d in range(CHUNK)]
            for c in range(stage // CHUNK):
                t = at * stage + c * CHUNK
                qc = filtered(qx, 0, h, t, CHUNK)
                base = h * tokens + t
                g = [g_s[row(base + i), :] for i in range(CHUNK)]
                for i in range(CHUNK):
                    y_s[row(base + i), :] = tree_sum(tap[d] * g[i - d] for d in range(i + 1))
                    qc_s[row(base + i), :] = qc[i]
            nh, na = following(h, at)
            spread(qbuf, qx, nh, na)
            return carry

        lax.fori_loop(0, stages, step, 0)

    def convert(h, t, values):
        tiles = jnp.swapaxes(jnp.stack(values), 0, 1)
        for s in range(SUBS):
            at = (h * SUBS + s) * LANES
            out_ref[pl.ds(pl.multiple_of(t, 2 * CHUNK), 2 * CHUNK), at : at + LANES] = tiles[s].astype(BF16)

    def finish(h):
        def waits(i, carry):
            owner = first + i

            @pl.when(owner != me)
            def _():
                got_back(h, owner).wait_recv()

            return carry

        @pl.when(me > 1)
        def _():
            lax.fori_loop(0, owners, waits, 0)

        @pl.when(me == 1)
        def _():
            send_direct(h).wait_recv()

        def step(at, carry):
            entry = list(carry)
            for p in range(4):
                t = (at * 4 + p) * 2 * CHUNK
                values = []
                for c in range(2):
                    for i in range(CHUNK):
                        here = row(h * tokens + t + c * CHUNK + i)
                        total = chain_sum((w_s[row((h * CHUNK + i) * modes + n), :] * entry[n] for n in range(modes)), 2)
                        values.append(qc_s[here, :] * (y_s[here, :] + total))
                    entry = [
                        a8[row(h * modes + n), :] * entry[n]
                        + h_s[row((h * chunks + (at * 4 + p) * 2 + c) * modes + n), :]
                        for n in range(modes)
                    ]
                convert(h, t, values)
            return tuple(entry)

        lax.fori_loop(0, pairs // 4, step, tuple(inc[row(h * modes + n), :] for n in range(modes)))

    loads[1, 0, 0].wait()
    loads[2, 0, 0].wait()
    spread(kbuf, kx, 0, 0)
    spread(vbuf, vx, 0, 0)
    @pl.when(me >= 6)
    def _():
        open_halo()

    for h in range(halves):
        states(h)
    for h in range(1, halves):
        correct(h)
        share(h)
    @pl.when(owning_here)
    def _():
        for h in range(halves):
            took(h)

    loads[0, 0, 0].wait()
    spread(qbuf, qx, 0, 0)
    for h in range(halves):
        margin(qx, 0, h)
    for h in range(halves):
        local(h)

    for h in range(halves):
        finish(h)

    @pl.when(me < last)
    def _():
        halo_copy.wait_send()

    def sent_ends(i, carry):
        owner = first + i

        @pl.when(owner != me)
        def _():
            for h in range(halves):
                send_ends(h, owner).wait_send()

        return carry

    def sent_back(q, carry):
        @pl.when(q != me)
        def _():
            for h in range(halves):
                send_back(h, q).wait_send()

        return carry

    @pl.when(me < last)
    def _():
        lax.fori_loop(0, owners, sent_ends, 0)

    @pl.when(owning_here)
    def _():
        lax.fori_loop(2, parts, sent_back, 0)

    @pl.when(me == 0)
    def _():
        for h in range(halves):
            send_direct(h).wait_send()


def per_device(query_proj, key_proj, value_proj, short_weight, decay_rate, residue, skip_gain):
    parts = lax.axis_size("ctx")
    tokens, channels = query_proj.shape
    modes = decay_rate.shape[0]
    halves = channels // WIDE
    owners = owning(parts)[1]
    own = modes // owners
    any_space = pl.BlockSpec(memory_space=pltpu.HBM)
    vm = pltpu.VMEM
    dma = pltpu.SemaphoreType.DMA

    def regs(count):
        return vm((count * SUBS, LANES), F32)

    return pl.pallas_call(
        functools.partial(layer_kernel, parts),
        out_shape=pltpu.VMEM((tokens, channels), BF16),
        in_specs=[any_space] * 7,
        out_specs=pl.BlockSpec(memory_space=pltpu.VMEM),
        scratch_shapes=[
            vm((tokens, channels), BF16),
            vm((tokens, channels), BF16),
            vm((tokens, channels), BF16),
            vm((3, EDGE, channels), BF16),
            vm(short_weight.shape, F32),
            vm(decay_rate.shape, F32),
            vm(residue.shape, F32),
            vm((1, channels), F32),
            regs((halves + 1) * (tokens + 2)),
            regs((halves + 1) * (tokens + 2)),
            regs((halves + 1) * (tokens + 2)),
            regs(3 * halves * 2 + SUBS),
            regs(3 * halves * 2),
            regs(halves * 9 + SUBS),
            regs(halves * modes),
            regs(halves * modes),
            regs(halves + 1),
            regs(halves * modes),
            regs(halves * modes),
            regs(halves * modes),
            regs(halves * modes),
            regs(halves * modes),
            regs(halves * CHUNK * modes),
            regs(halves * CHUNK),
            regs(halves * tokens),
            regs(halves * tokens // CHUNK * modes),
            regs(halves * tokens),
            regs(halves * tokens),
            regs(halves * modes),
            regs(halves * parts * own),
            regs(halves * parts * own),
            regs(halves * modes),
            dma((5 * halves,)),
            dma((3,)),
            dma((4,)),
            dma((2,)),
            dma((2 * halves,)),
            dma((halves * owners,)),
            dma((halves * parts,)),
            dma((halves * parts,)),
            dma((halves * owners,)),
        ],
        compiler_params=pltpu.CompilerParams(
            collective_id=0, has_side_effects=True, vmem_limit_bytes=62 * 1024 * 1024
        ),
    )(
        query_proj, key_proj, value_proj, short_weight, decay_rate, residue,
        skip_gain.reshape(1, channels),
    )


def solution(mesh):
    rows = P(("group", "ctx"), None)
    return jax.shard_map(
        per_device,
        mesh=mesh,
        in_specs=(rows, rows, rows, P(), P(), P(), P()),
        out_specs=rows,
        check_vma=False,
    )
```

```python
import functools

import jax
import jax.numpy as jnp
from jax import lax
from jax.experimental import pallas as pl
from jax.experimental.pallas import tpu as pltpu
from jax.sharding import PartitionSpec as P

MESH = pl.DeviceIdType.MESH
F32 = jnp.float32
BF16 = jnp.bfloat16
LANES = 128
SUBS = 8
WIDE = SUBS * LANES
CHUNK = 8
EDGE = 16


def owning(parts):
    return parts // 4, parts // 2


def tree_sum(terms):
    terms = list(terms)
    while len(terms) > 1:
        half = len(terms) // 2
        rest = terms[2 * half :]
        terms = [terms[i] + terms[i + half] for i in range(half)] + rest
    return terms[0]


def chain_sum(terms, lanes):
    totals = []
    for i, term in enumerate(terms):
        if i < lanes:
            totals.append(term)
        else:
            totals[i % lanes] = totals[i % lanes] + term
    return tree_sum(totals)


def layer_kernel(
    parts, q_hbm, k_hbm, v_hbm, sw_hbm, rate_hbm, res_hbm, skip_hbm, out_ref,
    qbuf, kbuf, vbuf, edge, sw, rate, res, skip,
    qx, kx, vx, tail, halo, sw_t, rate_t, res_t, skip_t,
    a1, a6, a8, a248, a256, w_s, taps, g_s, h_s, y_s, qc_s,
    ends, got, back, inc,
    load_sem, edge_sem, par_sem, halo_sem, direct_sem, send_a, recv_a, send_b, recv_b,
):
    tokens, channels = qbuf.shape
    modes = rate.shape[0]
    halves = channels // WIDE
    first, owners = owning(parts)
    own = modes // owners
    last = parts - 1
    chunks = tokens // CHUNK
    pairs = chunks // 2
    span = tokens + 2
    stage = 4 * EDGE
    stages = tokens // stage
    me = lax.axis_index("ctx")
    owning_here = jnp.logical_and(me >= first, me < first + owners)
    barrier = pltpu.get_barrier_semaphore()

    def row(i, count=1):
        start = i * SUBS
        if not isinstance(start, int):
            start = pl.multiple_of(start, SUBS)
        return pl.ds(start, count * SUBS)

    edge_copies = []
    for m, src in enumerate((q_hbm, k_hbm, v_hbm)):
        edge_copies.append(pltpu.make_async_copy(src.at[pl.ds(tokens - EDGE, EDGE)], edge.at[m], edge_sem.at[m]))
    par_copies = []
    for i, (src, dst) in enumerate(((rate_hbm, rate), (res_hbm, res), (sw_hbm, sw), (skip_hbm, skip))):
        par_copies.append(pltpu.make_async_copy(src, dst, par_sem.at[i]))
    loads = {}
    order = []

    def load(m, src, dst, h, part, first, count):
        at = (pl.ds(first, count), pl.ds(h * WIDE, WIDE))
        loads[m, h, part] = pltpu.make_async_copy(src.at[at], dst.at[at], load_sem.at[len(order)])
        order.append(loads[m, h, part])

    for h in range(halves):
        for part, begin, count in ((0, 0, stage), (1, stage, tokens - stage)):
            load(1, k_hbm, kbuf, h, part, begin, count)
            load(2, v_hbm, vbuf, h, part, begin, count)
    for h in range(halves):
        load(0, q_hbm, qbuf, h, 0, 0, tokens)
    early = [loads[m, 0, part] for part in (0, 1) for m in (1, 2)]
    late = [loads[m, h, part] for h in range(1, halves) for part in (0, 1) for m in (1, 2)]
    late += [loads[0, h, 0] for h in range(halves)]
    for c in par_copies + early[:2] + edge_copies + early[2:]:
        c.start()

    halo[...] = jnp.zeros(halo.shape, F32)
    inc[...] = jnp.zeros(inc.shape, F32)

    def greet(peer, carry=0):
        @pl.when(peer != me)
        def _():
            pl.semaphore_signal(barrier, inc=1, device_id={"ctx": peer}, device_id_type=MESH)

        return carry

    def owns(x):
        return jnp.logical_and(x >= first, x < first + owners)

    lax.fori_loop(jnp.where(owning_here, 0, first), jnp.where(owning_here, parts, first + owners), greet, 0)

    @pl.when(jnp.logical_and(jnp.logical_not(owning_here), jnp.logical_and(me > 0, jnp.logical_not(owns(me - 1)))))
    def _():
        greet(me - 1)

    for dst in (qx, kx, vx):
        for h in range(halves):
            dst[row(h * span, 2), :] = jnp.zeros((2 * SUBS, LANES), F32)

    for c in par_copies:
        c.wait()
    for h in range(halves):
        for s in range(SUBS):
            at = (h * SUBS + s) * LANES
            cols = slice(at, at + LANES)
            rate_t[pl.ds(h * modes * SUBS + s, modes, stride=SUBS), :] = rate[:, cols]
            res_t[pl.ds(h * modes * SUBS + s, modes, stride=SUBS), :] = res[:, cols]
            for m in range(3):
                sw_t[pl.ds((h * 3 + m) * 3 * SUBS + s, 3, stride=SUBS), :] = sw[m, :, cols]
            skip_t[h * SUBS + s : h * SUBS + s + 1, :] = skip[0:1, cols]

    def constants(h, carry):
        zero_lag, sums = [], [[] for _ in range(CHUNK)]
        for n in range(modes):
            at = row(h * modes + n)
            negative = -rate_t[at, :]
            weight = res_t[at, :]
            one = jnp.exp(negative)
            a1[at, :] = one
            a6[at, :] = jnp.exp(negative * float(CHUNK - 2))
            a8[at, :] = jnp.exp(negative * float(CHUNK))
            a248[at, :] = jnp.exp(negative * float(tokens - CHUNK))
            a256[at, :] = jnp.exp(negative * float(tokens))
            zero_lag.append(weight)
            for i in range(CHUNK):
                weight = weight * one
                w_s[row((h * CHUNK + i) * modes + n), :] = weight
                sums[i].append(weight)
        taps[row(h * CHUNK), :] = tree_sum(zero_lag) + skip_t[row(h), :]
        for d in range(1, CHUNK):
            taps[row(h * CHUNK + d), :] = tree_sum(sums[d - 1])
        return carry

    lax.fori_loop(0, halves, constants, 0)
    for c in late:
        c.start()

    for c in edge_copies:
        c.wait()
    for m in range(3):
        for h in range(halves):
            for s in range(SUBS):
                at = (h * SUBS + s) * LANES
                rows = edge[m, :, at : at + LANES].astype(F32)
                tail[pl.ds((m * halves + h) * 2 * SUBS + s, 2, stride=SUBS), :] = rows[EDGE - 2 :, :]

    def send_halo(i, first_row, count):
        return pltpu.make_async_remote_copy(
            src_ref=tail.at[row(first_row, count)], dst_ref=halo.at[row(first_row, count)],
            send_sem=halo_sem.at[2 * i], recv_sem=halo_sem.at[2 * i + 1],
            device_id={"ctx": lax.rem(me + 1, parts)}, device_id_type=MESH,
        )

    halo_copy = send_halo(0, 2 * halves, 4 * halves)
    query_copy = send_halo(1, 0, 2 * halves)

    def open_halo():
        to_next = jnp.logical_and(me < last, jnp.logical_not(owns(me + 1)))
        pl.semaphore_wait(barrier, jnp.where(owning_here, last, owners + jnp.where(to_next, 1, 0)))

        @pl.when(me < last)
        def _():
            halo_copy.start()
            query_copy.start()

    def spread(buf, dst, h, at):
        t = at * stage
        source = jnp.minimum(h, halves - 1) if not isinstance(h, int) else min(h, halves - 1)
        for u in range(0, stage, EDGE):
            rows = pl.ds(t + u if isinstance(t, int) else pl.multiple_of(t + u, EDGE), EDGE)
            base = (h * span + 2 + t + u) * SUBS
            for s in range(SUBS):
                lane = source * WIDE + s * LANES
                cols = pl.ds(lane if isinstance(lane, int) else pl.multiple_of(lane, LANES), LANES)
                dst[pl.ds(base + s, EDGE, stride=SUBS), :] = buf[rows, cols].astype(F32)

    def close_halo():
        @pl.when(me > 0)
        def _():
            halo_copy.wait_recv()

    def following(h, at):
        last = at == stages - 1
        return jnp.where(last, h + 1, h), jnp.where(last, 0, at + 1)

    def filtered(ref, m, h, t, count):
        base = h * span + t
        x = [ref[row(base + i), :] for i in range(count + 2)]
        w = [sw_t[row((h * 3 + m) * 3 + lag), :] for lag in range(3)]
        return [w[0] * x[i + 2] + w[1] * x[i + 1] + w[2] * x[i] for i in range(count)]

    def states(h):
        ends[row(h * modes, modes), :] = jnp.zeros((modes * SUBS, LANES), F32)

        def step(at, carry):
            @pl.when(at == 0)
            def _():
                loads[1, h, 1].wait()
                loads[2, h, 1].wait()

            if h + 1 < halves:
                @pl.when(at == stages - 1)
                def _():
                    loads[1, h + 1, 0].wait()
                    loads[2, h + 1, 0].wait()

            total = [ends[row(h * modes + n), :] for n in range(modes)]
            for p in range(stage // (2 * CHUNK)):
                t = at * stage + p * 2 * CHUNK
                kc = filtered(kx, 1, h, t, 2 * CHUNK)
                vc = filtered(vx, 2, h, t, 2 * CHUNK)
                g = [a * b for a, b in zip(kc, vc)]
                for i in range(2 * CHUNK):
                    g_s[row(h * tokens + t + i), :] = g[i]
                for n in range(modes):
                    a = a1[row(h * modes + n), :]
                    factor = a8[row(h * modes + n), :]
                    for c in range(2):
                        local = g[c * CHUNK]
                        for i in range(1, CHUNK):
                            local = a * local + g[c * CHUNK + i]
                        h_s[row((h * chunks + t // CHUNK + c) * modes + n), :] = local
                        total[n] = factor * total[n] + local
            for n in range(modes):
                ends[row(h * modes + n), :] = total[n]
            nh, na = following(h, at)
            spread(kbuf, kx, nh, na)
            spread(vbuf, vx, nh, na)
            if h == 0:
                @pl.when(at == jnp.where(me < 2, stages - 1, jnp.where(me < 6, 0, -1)))
                def _():
                    open_halo()

            if h == 1:
                @pl.when(at == jnp.where(me < 6, 1, 0))
                def _():
                    close_halo()
                    correct(0)
                    share(0)

            return carry

        lax.fori_loop(0, stages, step, 0)

    def margin(dst, m, h):
        dst[row(h * span, 2), :] = halo[row((m * halves + h) * 2, 2), :]

    def correct(h):
        margin(kx, 1, h)
        margin(vx, 2, h)
        g = [a * b for a, b in zip(filtered(kx, 1, h, 0, 2), filtered(vx, 2, h, 0, 2))]
        change = [g[i] - g_s[row(h * tokens + i), :] for i in range(2)]
        for i in range(2):
            g_s[row(h * tokens + i), :] = g[i]
        for n in range(modes):
            at = row(h * modes + n)
            extra = a6[at, :] * (a1[at, :] * change[0] + change[1])
            first = row(h * chunks * modes + n)
            h_s[first, :] = h_s[first, :] + extra
            ends[at, :] = ends[at, :] + a248[at, :] * extra

    def modes_of(h, owner):
        return row(h * modes + (owner - first) * own, own)

    def sums(h, device):
        return row((h * parts + device) * own, own)

    def send_ends(h, owner):
        return pltpu.make_async_remote_copy(
            src_ref=ends.at[modes_of(h, owner)], dst_ref=got.at[sums(h, me)],
            send_sem=send_a.at[h * owners + owner - first], recv_sem=recv_a.at[h * parts + me],
            device_id={"ctx": owner}, device_id_type=MESH,
        )

    def got_ends(h, p):
        return pltpu.make_async_remote_copy(
            src_ref=ends.at[modes_of(h, first)], dst_ref=got.at[sums(h, p)],
            send_sem=send_a.at[h * owners], recv_sem=recv_a.at[h * parts + p],
            device_id={"ctx": p}, device_id_type=MESH,
        )

    def send_back(h, q):
        return pltpu.make_async_remote_copy(
            src_ref=back.at[sums(h, q)], dst_ref=inc.at[modes_of(h, me)],
            send_sem=send_b.at[h * parts + q], recv_sem=recv_b.at[h * owners + me - first],
            device_id={"ctx": q}, device_id_type=MESH,
        )

    def got_back(h, owner):
        return pltpu.make_async_remote_copy(
            src_ref=back.at[sums(h, 0)], dst_ref=inc.at[modes_of(h, owner)],
            send_sem=send_b.at[h * parts], recv_sem=recv_b.at[h * owners + owner - first],
            device_id={"ctx": owner}, device_id_type=MESH,
        )

    def send_direct(h):
        return pltpu.make_async_remote_copy(
            src_ref=ends.at[row(h * modes, modes)], dst_ref=inc.at[row(h * modes, modes)],
            send_sem=direct_sem.at[2 * h], recv_sem=direct_sem.at[2 * h + 1],
            device_id={"ctx": lax.rem(me + 1, parts)}, device_id_type=MESH,
        )

    def share(h):
        def body(i, carry):
            owner = first + lax.rem(me + i, owners)

            @pl.when(owner != me)
            def _():
                send_ends(h, owner).start()

            return carry

        @pl.when(me < last)
        def _():
            lax.fori_loop(0, owners, body, 0)

        @pl.when(me == 0)
        def _():
            send_direct(h).start()

        @pl.when(owning_here)
        def _():
            got[sums(h, me), :] = ends[modes_of(h, me), :]

    def took(h):
        factor = a256[modes_of(h, me), :]

        def body(p, total):
            @pl.when(p != me)
            def _():
                got_ends(h, p).wait_recv()

            total = factor * total + got[sums(h, p), :]
            q = p + 1

            @pl.when(jnp.logical_and(q != me, q > 1))
            def _():
                back[sums(h, q), :] = total
                send_back(h, q).start()

            @pl.when(q == me)
            def _():
                inc[modes_of(h, me), :] = total

            return total

        lax.fori_loop(0, last, body, jnp.zeros((own * SUBS, LANES), F32))

    def local(h):
        def step(at, carry):
            if h + 1 < halves:
                @pl.when(at == stages - 1)
                def _():
                    loads[0, h + 1, 0].wait()

            tap = [taps[row(h * CHUNK + d), :] for d in range(CHUNK)]
            for c in range(stage // CHUNK):
                t = at * stage + c * CHUNK
                qc = filtered(qx, 0, h, t, CHUNK)
                base = h * tokens + t
                g = [g_s[row(base + i), :] for i in range(CHUNK)]
                for i in range(CHUNK):
                    y_s[row(base + i), :] = tree_sum(tap[d] * g[i - d] for d in range(i + 1))
                    qc_s[row(base + i), :] = qc[i]
            nh, na = following(h, at)
            spread(qbuf, qx, nh, na)
            return carry

        lax.fori_loop(0, stages, step, 0)

    def convert(h, t, values):
        tiles = jnp.swapaxes(jnp.stack(values), 0, 1)
        for s in range(SUBS):
            at = (h * SUBS + s) * LANES
            out_ref[pl.ds(pl.multiple_of(t, 2 * CHUNK), 2 * CHUNK), at : at + LANES] = tiles[s].astype(BF16)

    def finish(h):
        def waits(i, carry):
            owner = first + i

            @pl.when(owner != me)
            def _():
                got_back(h, owner).wait_recv()

            return carry

        @pl.when(me > 1)
        def _():
            lax.fori_loop(0, owners, waits, 0)

        @pl.when(me == 1)
        def _():
            send_direct(h).wait_recv()

        def step(at, carry):
            entry = list(carry)
            for p in range(4):
                t = (at * 4 + p) * 2 * CHUNK
                values = []
                for c in range(2):
                    for i in range(CHUNK):
                        here = row(h * tokens + t + c * CHUNK + i)
                        total = chain_sum((w_s[row((h * CHUNK + i) * modes + n), :] * entry[n] for n in range(modes)), 2)
                        values.append(qc_s[here, :] * (y_s[here, :] + total))
                    entry = [
                        a8[row(h * modes + n), :] * entry[n]
                        + h_s[row((h * chunks + (at * 4 + p) * 2 + c) * modes + n), :]
                        for n in range(modes)
                    ]
                convert(h, t, values)
            return tuple(entry)

        lax.fori_loop(0, pairs // 4, step, tuple(inc[row(h * modes + n), :] for n in range(modes)))

    loads[1, 0, 0].wait()
    loads[2, 0, 0].wait()
    spread(kbuf, kx, 0, 0)
    spread(vbuf, vx, 0, 0)
    @pl.when(me >= 6)
    def _():
        open_halo()

    for h in range(halves):
        states(h)
    for h in range(1, halves):
        correct(h)
        share(h)
    @pl.when(owning_here)
    def _():
        for h in range(halves):
            took(h)

    loads[0, 0, 0].wait()
    spread(qbuf, qx, 0, 0)
    @pl.when(me > 0)
    def _():
        query_copy.wait_recv()

    for h in range(halves):
        margin(qx, 0, h)
    for h in range(halves):
        local(h)

    for h in range(halves):
        finish(h)

    @pl.when(me < last)
    def _():
        halo_copy.wait_send()
        query_copy.wait_send()

    def sent_ends(i, carry):
        owner = first + i

        @pl.when(owner != me)
        def _():
            for h in range(halves):
                send_ends(h, owner).wait_send()

        return carry

    def sent_back(q, carry):
        @pl.when(q != me)
        def _():
            for h in range(halves):
                send_back(h, q).wait_send()

        return carry

    @pl.when(me < last)
    def _():
        lax.fori_loop(0, owners, sent_ends, 0)

    @pl.when(owning_here)
    def _():
        lax.fori_loop(2, parts, sent_back, 0)

    @pl.when(me == 0)
    def _():
        for h in range(halves):
            send_direct(h).wait_send()


def per_device(query_proj, key_proj, value_proj, short_weight, decay_rate, residue, skip_gain):
    parts = lax.axis_size("ctx")
    tokens, channels = query_proj.shape
    modes = decay_rate.shape[0]
    halves = channels // WIDE
    owners = owning(parts)[1]
    own = modes // owners
    any_space = pl.BlockSpec(memory_space=pltpu.HBM)
    vm = pltpu.VMEM
    dma = pltpu.SemaphoreType.DMA

    def regs(count):
        return vm((count * SUBS, LANES), F32)

    return pl.pallas_call(
        functools.partial(layer_kernel, parts),
        out_shape=pltpu.VMEM((tokens, channels), BF16),
        in_specs=[any_space] * 7,
        out_specs=pl.BlockSpec(memory_space=pltpu.VMEM),
        scratch_shapes=[
            vm((tokens, channels), BF16),
            vm((tokens, channels), BF16),
            vm((tokens, channels), BF16),
            vm((3, EDGE, channels), BF16),
            vm(short_weight.shape, F32),
            vm(decay_rate.shape, F32),
            vm(residue.shape, F32),
            vm((1, channels), F32),
            regs((halves + 1) * (tokens + 2)),
            regs((halves + 1) * (tokens + 2)),
            regs((halves + 1) * (tokens + 2)),
            regs(3 * halves * 2 + SUBS),
            regs(3 * halves * 2),
            regs(halves * 9 + SUBS),
            regs(halves * modes),
            regs(halves * modes),
            regs(halves + 1),
            regs(halves * modes),
            regs(halves * modes),
            regs(halves * modes),
            regs(halves * modes),
            regs(halves * modes),
            regs(halves * CHUNK * modes),
            regs(halves * CHUNK),
            regs(halves * tokens),
            regs(halves * tokens // CHUNK * modes),
            regs(halves * tokens),
            regs(halves * tokens),
            regs(halves * modes),
            regs(halves * parts * own),
            regs(halves * parts * own),
            regs(halves * modes),
            dma((5 * halves,)),
            dma((3,)),
            dma((4,)),
            dma((4,)),
            dma((2 * halves,)),
            dma((halves * owners,)),
            dma((halves * parts,)),
            dma((halves * parts,)),
            dma((halves * owners,)),
        ],
        compiler_params=pltpu.CompilerParams(
            collective_id=0, has_side_effects=True, vmem_limit_bytes=62 * 1024 * 1024
        ),
    )(
        query_proj, key_proj, value_proj, short_weight, decay_rate, residue,
        skip_gain.reshape(1, channels),
    )


def solution(mesh):
    rows = P(("group", "ctx"), None)
    return jax.shard_map(
        per_device,
        mesh=mesh,
        in_specs=(rows, rows, rows, P(), P(), P(), P()),
        out_specs=rows,
        check_vma=False,
    )
```
